128 devices in a mesh: ent: 32 (over x_hi, z, y), sec: 4 (over x_lo, core).
Axes of the slice: x: 4 (x_hi: 2, x_lo: 2; x = x_hi * 2 + x_lo), y: 4, z: 4, core: 2. Of those that a mesh axis runs over, the one named last changes fastest.
Arguments:
- features: bfloat16 [4096, 256], P('ent'), may hold values from -6 to 6
- theta: bfloat16 [256, 256], replicated, may hold values from -3 to 3
- section_weight: float32 [65536], P(('ent', 'sec')), may hold values from 0.5 to 2
- pair_rows: int32 [128, 32, 512], P(('ent', 'sec')), may hold values from 0 to 511
- pair_cols: int32 [128, 32, 512], P(('ent', 'sec')), may hold values from 0 to 127
- pair_counts: int32 [128, 32], P(('ent', 'sec')), may hold values from 0 to 512, as said below
- cotangent: bfloat16 [4096, 256], P('ent'), may hold values from -24 to 24
Outputs:
- activated: bfloat16 [4096, 256], P('ent')
- grad_features: bfloat16 [4096, 256], P('ent')
- grad_theta: float32 [256, 256], replicated
- grad_weight: float32 [65536], P(('ent', 'sec'))
The draws below stay inside these ranges and needn't reach their ends.
Inputs may be any that keep to these rules, and one draw needn't show every extreme that they name: Only the first pair_counts[k, j] slots of shard k and block j are used; some shard uses all 512 slots of some block.
All inputs are finite; a program needn't handle non-finite values.
Results may differ from the reference program's by a relative error of at most 0.0059.
Values may be sent and summed in bfloat16 or wider, within the bound.
A program may use at most 64 MiB of HBM per device.

```python
import math
import jax
import jax.numpy as jnp
from jax import lax

F = 256
ENT_DEV = 128
SEC_DEV = 512
PAIRS = 512
ENTS = 4096
SHARDS = 128
SECTIONS = 65536
N_ENT = 32


def draw_pair_counts(key, part):
    level_key, hot_key, jitter_key, full_key = jax.random.split(key, 4)
    levels = jax.random.randint(level_key, (N_ENT,), 0, 4)
    hot_block = jax.random.randint(hot_key, (), 0, N_ENT)
    block_ids = jnp.arange(N_ENT, dtype=jnp.int32)
    levels = jnp.where(block_ids == hot_block, 3, levels)
    block_load = PAIRS * jnp.left_shift(jnp.int32(1), levels) // 8
    jitter = jax.random.randint(jitter_key, (SHARDS, N_ENT), 0, PAIRS // 16 + 1)
    full_shard = jax.random.randint(full_key, (), 0, SHARDS)
    shard_ids = jnp.arange(SHARDS, dtype=jnp.int32)
    pinned = (shard_ids[:, None] == full_shard) & (block_ids[None, :] == hot_block)
    jitter = jnp.where(pinned, 0, jitter)
    return jnp.maximum(block_load[None, :] - jitter, 0).astype(jnp.int32)


def touch_ends(result, key, smallest, high):
    extent = result.shape
    index_at = [jax.random.randint(jax.random.fold_in(key, axis), (), 0, extent[axis]) for axis in range(len(extent))]
    result = result.at[tuple(index_at)].set(smallest)
    longest = extent.index(max(extent))
    index_at[longest] = (index_at[longest] + 1) % extent[longest]
    return result.at[tuple(index_at)].set(high)


def steps_of(rng, dims, cuts, least, top_value):
    level = 1.0
    for dim, blocks in cuts:
        draws = jax.random.uniform(jax.random.fold_in(jax.random.fold_in(rng, 6), dim), (blocks,), jnp.float32, least / len(cuts), top_value / len(cuts))
        level = level * jnp.repeat(jnp.exp(draws), dims[dim] // blocks).reshape((-1,) + (1,) * (len(dims) - 1 - dim))
    return level


def centred(own_key, extent, scale, bound, cuts=(), kind=jnp.bfloat16):
    drawn = jax.random.normal(own_key, extent, jnp.float32) * scale
    if len(cuts) > 0:
        drawn = steps_of(own_key, extent, cuts, -0.22, 0.18) * drawn
    return jnp.clip(drawn, min=-bound, max=bound).astype(kind)


def setup_inputs(seed: int = 0) -> dict:
    streams_of = jax.random.split(jax.random.key(seed), 8)
    features = centred(streams_of[0], (ENTS, F), 1.0, 6.0, ((0, 32),))
    theta = centred(streams_of[1], (F, F), 0.5, 3.0)
    section_weight = jnp.clip(jnp.exp(math.log(2.0) - 1.3862944 * jax.random.uniform(streams_of[2], (SECTIONS,), jnp.float32) ** steps_of(streams_of[2], (SECTIONS,), ((0, 128),), -0.2, 0.2)), 0.5, 2.0)
    pair_rows = touch_ends(jax.random.randint(streams_of[3], (SHARDS, N_ENT, PAIRS), 0, SEC_DEV), jax.random.fold_in(streams_of[3], 1), 0, SEC_DEV - 1).astype(jnp.int32)
    pair_cols = touch_ends(jax.random.randint(streams_of[4], (SHARDS, N_ENT, PAIRS), 0, ENT_DEV), jax.random.fold_in(streams_of[4], 1), 0, ENT_DEV - 1).astype(jnp.int32)
    pair_counts = draw_pair_counts(jax.random.fold_in(streams_of[7], 71), 0)
    cotangent = centred(streams_of[6], (ENTS, F), 4.0, 24.0, ((0, 32),))
    return {"features": features, "theta": theta, "section_weight": section_weight, "pair_rows": pair_rows, "pair_cols": pair_cols, "pair_counts": pair_counts, "cotangent": cotangent}


def reference(features, theta, section_weight, pair_rows, pair_cols, pair_counts, cotangent):
    shards, blocks_count, slot_count = pair_rows.shape
    usable = (jnp.arange(slot_count, dtype=jnp.int32)[None, None, :] < pair_counts[:, :, None]).astype(jnp.float32)
    entity_index = (jnp.arange(blocks_count, dtype=jnp.int32)[None, :, None] * ENT_DEV + pair_cols).reshape(shards, -1).astype(jnp.int32)
    row_index = pair_rows.reshape(shards, -1).astype(jnp.int32)
    usable_flat = usable.reshape(shards, -1)
    entity_degree = jnp.zeros((ENTS,), jnp.float32).at[entity_index.reshape(-1)].add(usable_flat.reshape(-1))
    entity_scale = lax.rsqrt(1.0 + entity_degree)[:, None]

    def count_rows(rows_here, live_here):
        return jnp.zeros((SEC_DEV,), jnp.float32).at[rows_here].add(live_here)
    sec_count = jax.vmap(count_rows)(row_index, usable_flat).reshape(-1)
    section_scale = (section_weight / (1.0 + sec_count))[:, None]

    def gather_sections(values):

        def per_shard(packed):
            rows_here, cols_here, live_here = packed
            picked = values[cols_here].astype(jnp.float32) * live_here[:, None]
            return jnp.zeros((SEC_DEV, values.shape[1]), jnp.float32).at[rows_here].add(picked)
        return lax.map(per_shard, (row_index, entity_index, usable_flat)).reshape(-1, values.shape[1])

    def scatter_entities(messages):
        shard_rows = messages.reshape(shards, SEC_DEV, -1)

        def add_shard(running, packed):
            rows_here, cols_here, live_here, rows_block = packed
            picked = rows_block[rows_here].astype(jnp.float32) * live_here[:, None]
            return (running.at[cols_here].add(picked), None)
        running, _ = lax.scan(add_shard, jnp.zeros((ENTS, messages.shape[1]), jnp.float32), (row_index, entity_index, usable_flat, shard_rows))
        return running
    projected = jnp.dot(features, theta, preferred_element_type=jnp.float32)
    scaled = (entity_scale * projected).astype(jnp.bfloat16)
    gathered = gather_sections(scaled)
    messages = (section_scale * gathered).astype(jnp.bfloat16)
    collected = scatter_entities(messages)
    preact = entity_scale * collected
    activated = jax.nn.silu(preact).astype(jnp.bfloat16)
    sigmoid_pre = jax.nn.sigmoid(preact)
    grad_pre = cotangent.astype(jnp.float32) * sigmoid_pre * (1.0 + preact * (1.0 - sigmoid_pre))
    back_scaled = (entity_scale * grad_pre).astype(jnp.bfloat16)
    back_gathered = gather_sections(back_scaled)
    grad_weight = lax.optimization_barrier(jnp.sum(gathered * back_gathered, axis=1)) / (1.0 + sec_count)
    back_messages = (section_scale * back_gathered).astype(jnp.bfloat16)
    back_collected = scatter_entities(back_messages)
    grad_proj = (entity_scale * back_collected).astype(jnp.bfloat16)
    grad_features = jnp.dot(grad_proj, theta.T, preferred_element_type=jnp.float32).astype(jnp.bfloat16)
    grad_theta = jnp.dot(features.T, grad_proj, preferred_element_type=jnp.float32)
    return (activated, grad_features, grad_theta, grad_weight)
```

```python
import jax
import jax.numpy as jnp
from jax import lax
from jax.experimental import pallas as pl
from jax.experimental.pallas import tpu as pltpu
from jax.sharding import PartitionSpec as P

F32 = jnp.float32
BF16 = jnp.bfloat16
MESH = pl.DeviceIdType.MESH
NT = (((1,), (1,)), ((), ()))
NN = (((1,), (0,)), ((), ()))
N_SEM = 160


def dot(a, b, dims):
    return lax.dot_general(a, b, dims, preferred_element_type=F32)


def split(v):
    hi = v.astype(BF16)
    return hi, (v - hi.astype(F32)).astype(BF16)


def layer(
    feat, theta, sw, rows, cols, counts, cot,
    act_o, gf_o, gt_o, gw_o,
    HT, HS, degs, degr, degc, degt, SW, INV, XF, XS, G, GR, GH, GL, GATH, MT, PF, PB,
    RB, CB, ACC, YS, YR, A2, XR, AS, AR, FS, FR, TH,
    T0, TZ, T1, TY, TX, T3, TS, ssem, rsem,
):
    e = lax.axis_index("ent")
    s = lax.axis_index("sec")
    core = lax.rem(s, 2)
    xl = lax.div(s, 2)
    xh = lax.div(e, 16)
    z = lax.rem(lax.div(e, 4), 4)
    y = lax.rem(e, 4)
    myx = xh * 2 + xl
    half = pl.multiple_of(core * 64, 64)
    other_half = pl.multiple_of((1 - core) * 64, 64)

    def dev(xh_, xl_, z_, y_):
        return (xh_ * 16 + z_ * 4 + y_, xl_ * 2 + core)

    sib = (e, xl * 2 + 1 - core)
    x_pair = dev(1 - xh, 1 - xl, z, y)
    x_far = dev(1 - xh, xl, z, y)
    x_same = dev(xh, 1 - xl, z, y)

    def mod4(v):
        return lax.rem(v + 4, 4)

    def z_dev(d):
        return dev(xh, xl, mod4(z + d), y)

    def y_dev(d):
        return dev(xh, xl, z, mod4(y + d))

    peers = [sib, x_pair, x_far, x_same] + [z_dev(d) for d in (1, 2, 3)] + [y_dev(d) for d in (1, 2, 3)]
    sent = []

    def send(src, dst, device):
        i = len(sent)
        copy = pltpu.make_async_remote_copy(
            src_ref=src, dst_ref=dst, send_sem=ssem.at[i], recv_sem=rsem.at[i],
            device_id=device, device_id_type=MESH,
        )
        copy.start()
        sent.append(copy)
        return copy

    def arrived(copies):
        for copy in copies:
            copy.wait_recv()

    barrier = pltpu.get_barrier_semaphore()
    for peer in peers:
        pl.semaphore_signal(barrier, inc=1, device_id=peer, device_id_type=MESH)

    slot_row = lax.broadcasted_iota(jnp.int32, (1, 512), 1)
    ent_iota = lax.broadcasted_iota(jnp.int32, (128, 512), 0)

    def col_table(j):
        live = slot_row < counts[0, j]
        col = jnp.where(live, cols[0, pl.ds(j, 1), :], -1)
        return jnp.where(ent_iota == col, 1.0, 0.0).astype(BF16)

    for p in range(2):
        XF[0, p, xh, z, y] = feat[pl.ds(half, 64), p * 128:(p + 1) * 128]
    TH[...] = theta[...].T

    pl.semaphore_wait(barrier, len(peers))

    def all_gather(ph, p):
        buf = XF.at[ph, p]
        axis_dev, ring_dev, ring = (y_dev, z_dev, z) if p == 0 else (z_dev, y_dev, y)

        def line(i):
            return buf.at[:, i] if p == 0 else buf.at[:, :, i]

        def part_line(i, lo):
            return buf.at[:, i, lo:lo + 2] if p == 0 else buf.at[:, lo:lo + 2, i]

        own = buf.at[xh, z, y]
        m = [send(own, own, x_pair)]
        yield
        arrived(m)
        own = buf.at[:, z, y]
        m = [send(own, own, axis_dev(d)) for d in (1, 3, 2)]
        yield
        arrived(m)
        m = [send(line(ring), line(ring), ring_dev(d)) for d in (1, 3)]
        yield
        arrived(m)
        below, above = mod4(ring - 1), mod4(ring + 1)
        m = [
            send(part_line(below, 0), part_line(below, 0), ring_dev(1)),
            send(part_line(above, 2), part_line(above, 2), ring_dev(3)),
        ]
        yield
        arrived(m)
        yield

    def degree_sum():
        m = [send(degs.at[0], degr.at[0], sib)]
        yield
        arrived(m)
        degs[1] = degs[0] + degr[0]
        m = [send(degs.at[1], degr.at[1 + i], d) for i, d in enumerate((x_pair, x_same, x_far))]
        yield
        arrived(m)
        degs[2] = degs[1] + degr[1] + degr[2] + degr[3]
        m = [send(degs.at[2], degr.at[3 + d], y_dev(d)) for d in (1, 3, 2)]
        yield
        arrived(m)
        degs[3] = degs[2] + degr[4] + degr[5] + degr[6]
        m = [send(degs.at[3], degr.at[6 + d], z_dev(d)) for d in (1, 3, 2)]
        yield
        arrived(m)
        degs[4] = degs[3] + degr[7] + degr[8] + degr[9]
        yield

    def step(gens):
        for g in gens:
            next(g, None)

    gathers = [all_gather(0, 0), all_gather(0, 1)]
    step(gathers)
    SW[0] = sw[...]
    sw_copy = send(SW.at[0], SW.at[1], sib)

    ones = jnp.ones((8, 512), BF16)

    def degree_block(j, carry):
        degs[0, pl.ds(j, 1), :] = dot(ones, col_table(j), NT)[0:1]
        return carry

    lax.fori_loop(0, 32, degree_block, 0)
    degrees = degree_sum()
    step([degrees] + gathers)

    sec_iota = lax.broadcasted_iota(jnp.int32, (512, 512), 0)

    def table_block(j, carry):
        row_hot = jnp.where(sec_iota == rows[0, pl.ds(j, 1), :], 1.0, 0.0).astype(BF16)
        block = dot(col_table(j), row_hot, NT).astype(BF16)
        HT[0, j] = block[0:64]
        HT[1, j] = block[64:128]
        return carry

    table_copies = []
    for k in range(8):
        lax.fori_loop(4 * k, 4 * k + 4, table_block, 0)
        table_copies.append(send(HT.at[1 - core, 4 * k:4 * k + 4], HS.at[4 * k:4 * k + 4], sib))
        step([degrees] + gathers)

    arrived(table_copies)
    arrived([sw_copy])

    degc[...] = jnp.zeros((128, 128), F32)
    degc[0:32, :] = lax.rsqrt(1.0 + degs[4])
    degt[...] = degc[...].T
    scales = degt[pl.ds(half, 64), :]
    own_lane = lax.broadcasted_iota(jnp.int32, (64, 128), 1) == e
    own_scale = jnp.sum(jnp.where(own_lane, scales, 0.0), axis=1, keepdims=True)

    for j in range(32):
        for p in range(2):
            v = XF[0, p, j // 16, (j // 4) % 4, j % 4].astype(F32)
            XS[p, j // 4, j % 4] = (v * scales[:, j:j + 1]).astype(BF16)

    def gather_sections(ph):
        width = 272 if ph == 0 else 256
        for k in range(2):
            G[ph, k, 0:width] = jnp.zeros((width, 512), F32)

        def chunk(kk, carry):
            if ph == 0:
                pieces = [XS[p, kk].reshape(256, 128) for p in range(2)]
            else:
                pieces = [XF[1, p, lax.div(kk, 4), lax.rem(kk, 4)].reshape(256, 128) for p in range(2)]
            xt = jnp.concatenate(pieces, axis=1).T
            if ph == 0:
                xt = jnp.concatenate([xt, jnp.ones((16, 256), BF16)], axis=0)
            own = HT[core, pl.ds(4 * kk, 4)].reshape(256, 512)
            sibs = HS[pl.ds(4 * kk, 4)].reshape(256, 512)
            G[ph, 0, 0:width] += dot(xt, own, NN)
            G[ph, 1, 0:width] += dot(xt, sibs, NN)
            return carry

        lax.fori_loop(0, 8, chunk, 0)
        m = [send(G.at[ph, k, 0:width], GR.at[ph, k, 0:width], sib) for k in (1, 0)]
        arrived(m)
        return [G[ph, k, 0:width] + GR[ph, 1 - k, 0:width] for k in range(2)]

    def scatter_entities(ph):
        def chunk(kk, carry):
            own = HT[core, pl.ds(4 * kk, 4)].reshape(256, 512)
            sibs = HS[pl.ds(4 * kk, 4)].reshape(256, 512)
            v = dot(own, MT[ph, 0], NT) + dot(sibs, MT[ph, 1], NT)
            a, b = lax.div(kk, 4), lax.rem(kk, 4)
            for p in range(2):
                piece = v[:, p * 128:(p + 1) * 128].reshape(4, 64, 128)
                PF[p, a, b] = piece
                PB[ph, p, a, b] = piece.astype(BF16)
            return carry

        lax.fori_loop(0, 8, chunk, 0)

    def reduce_scatter(ph, p, out):
        full, low = PF.at[p], PB.at[ph, p]
        ring_dev, axis_dev, ring, axis = (z_dev, y_dev, z, y) if p == 0 else (y_dev, z_dev, y, z)

        def lines(ref, i, lo):
            return ref.at[:, i, lo:lo + 2] if p == 0 else ref.at[:, lo:lo + 2, i]

        def tile(a, i, o):
            return full[a, i, o] if p == 0 else full[a, o, i]

        far, above, below = mod4(ring + 2), mod4(ring + 1), mod4(ring - 1)
        rb, cb = RB.at[ph, p], CB.at[ph, p]
        far_up = send(lines(low, far, 0), rb.at[0], ring_dev(1))
        far_down = send(lines(low, far, 2), rb.at[1], ring_dev(3))
        near_up = send(lines(low, above, 2), rb.at[2], ring_dev(1))
        near_down = send(lines(low, below, 0), rb.at[3], ring_dev(3))
        yield
        arrived([far_up])
        for a in range(2):
            for o in range(2):
                cb[0, a, o] = (tile(a, above, o) + rb[0, a, o].astype(F32)).astype(BF16)
        up = send(cb.at[0], rb.at[4], ring_dev(1))
        arrived([far_down])
        for a in range(2):
            for o in range(2):
                cb[1, a, o] = (tile(a, below, 2 + o) + rb[1, a, o].astype(F32)).astype(BF16)
        down = send(cb.at[1], rb.at[5], ring_dev(3))
        yield
        arrived([near_up, near_down, up, down])
        for a in range(2):
            for o in range(2):
                low_sum = tile(a, ring, o) + rb[3, a, o].astype(F32) + rb[4, a, o].astype(F32)
                high_sum = tile(a, ring, 2 + o) + rb[2, a, o].astype(F32) + rb[5, a, o].astype(F32)
                ACC[p, o, a] = low_sum
                ACC[p, 2 + o, a] = high_sum
                YS[ph, p, o, a] = low_sum.astype(BF16)
                YS[ph, p, 2 + o, a] = high_sum.astype(BF16)
        m = [send(YS.at[ph, p, mod4(axis + d)], YR.at[ph, p, d - 1], axis_dev(d)) for d in (2, 1, 3)]
        yield
        arrived(m)
        for a in range(2):
            v = ACC[p, axis, a]
            for i in range(3):
                v = v + YR[ph, p, i, a].astype(F32)
            A2[ph, p, a] = v
        m = [
            send(A2.at[ph, p, 1 - xh], XR.at[ph, p, myx], x_far),
            send(A2.at[ph, p, 1 - xh], XR.at[ph, p, myx], x_pair),
            send(A2.at[ph, p, xh], XR.at[ph, p, myx], x_same),
        ]
        XR[ph, p, myx] = A2[ph, p, xh]
        yield
        arrived(m)
        out[p] = (XR[ph, p, 0] + XR[ph, p, 1]) + (XR[ph, p, 2] + XR[ph, p, 3])
        yield

    totals = gather_sections(0)
    for k in range(2):
        g = totals[k]
        inverse = 1.0 / (1.0 + g[256:257])
        hi, lo = split(g[0:256])
        GH[k] = hi
        GL[k] = lo
        gathered = dot(TH[...], hi, NN) + dot(TH[...], lo, NN)
        if k == 0:
            GATH[...] = gathered
        INV[k] = inverse
        MT[0, k] = ((SW[k] * inverse) * gathered).astype(BF16)
    scatter_entities(0)

    collected = {}
    flows = [reduce_scatter(0, p, collected) for p in range(2)]
    for _ in range(5):
        step(flows)

    back = []
    for p in range(2):
        lanes = slice(p * 128, (p + 1) * 128)
        preact = own_scale * collected[p]
        sig = 1.0 / (1.0 + jnp.exp(-preact))
        AS[:, lanes] = (preact * sig).astype(BF16)
        grad = cot[pl.ds(half, 64), lanes].astype(F32) * sig * (1.0 + preact * (1.0 - sig))
        XF[1, p, xh, z, y] = (own_scale * grad).astype(BF16)
        back.append(all_gather(1, p))
        step([back[p]])
    act_copy = send(AS, AR, sib)
    for _ in range(4):
        step(back)
    act_o[pl.ds(half, 64), :] = AS[...]
    arrived([act_copy])
    act_o[pl.ds(other_half, 64), :] = AR[...]

    totals = gather_sections(1)
    for k in range(2):
        g = totals[k]
        if k == 0:
            gw_o[...] = jnp.sum(GATH[...] * g, axis=0, keepdims=True) * INV[0]
        MT[1, k] = ((SW[k] * INV[k]) * g).astype(BF16)
    scatter_entities(1)

    def theta_sum():
        rows_here = pl.ds(pl.multiple_of(core * 128, 128), 128)
        v = jnp.zeros((128, 256), F32)
        for k in range(2):
            v = v + dot(GH[k, rows_here, :], MT[1, k], NT) + dot(GL[k, rows_here, :], MT[1, k], NT)
        T0[...] = v.reshape(4, 4, 8, 256)
        m = [send(T0.at[mod4(z + d)], TZ.at[d - 1], z_dev(d)) for d in (2, 1, 3)]
        yield
        arrived(m)
        T1[...] = T0[z] + TZ[0] + TZ[1] + TZ[2]
        m = [send(T1.at[mod4(y + d)], TY.at[d - 1], y_dev(d)) for d in (2, 1, 3)]
        yield
        arrived(m)
        TX[myx] = T1[y] + TY[0] + TY[1] + TY[2]
        m = [send(TX.at[myx], TX.at[myx], d) for d in (x_far, x_pair, x_same)]
        yield
        arrived(m)
        T3[z, y] = (TX[0] + TX[1]) + (TX[2] + TX[3])
        m = [send(T3.at[z, y], T3.at[z, y], y_dev(d)) for d in (2, 1, 3)]
        yield
        arrived(m)
        m = [send(T3.at[z], T3.at[z], z_dev(d)) for d in (2, 1, 3)]
        yield
        arrived(m)
        m = [send(T3, TS, sib)]
        yield
        arrived(m)
        mine = pl.ds(pl.multiple_of(core * 128, 128), 128)
        theirs = pl.ds(pl.multiple_of((1 - core) * 128, 128), 128)
        gt_o[mine, :] = T3[...].reshape(128, 256)
        gt_o[theirs, :] = TS[...].reshape(128, 256)
        yield

    collected = {}
    flows = [reduce_scatter(1, p, collected) for p in range(2)]
    step(flows)
    flows.append(theta_sum())
    step(flows[2:])
    for _ in range(4):
        step(flows)

    proj = jnp.concatenate([own_scale * collected[p] for p in range(2)], axis=1)
    hi, lo = split(proj)
    FS[...] = (dot(hi, theta[...], NT) + dot(lo, theta[...], NT)).astype(BF16)
    grad_copy = send(FS, FR, sib)
    step(flows)
    gf_o[pl.ds(half, 64), :] = FS[...]
    arrived([grad_copy])
    gf_o[pl.ds(other_half, 64), :] = FR[...]
    step(flows)
    step(flows)
    assert len(sent) <= N_SEM
    for copy in sent:
        copy.wait_send()


def body(features, theta, section_weight, pair_rows, pair_cols, pair_counts, cotangent):
    vmem = pl.BlockSpec(memory_space=pltpu.VMEM)
    smem = pl.BlockSpec(memory_space=pltpu.SMEM)

    def buf(shape, dtype):
        return pltpu.VMEM(shape, dtype)

    outs = pl.pallas_call(
        layer,
        out_shape=(
            jax.ShapeDtypeStruct((128, 256), BF16),
            jax.ShapeDtypeStruct((128, 256), BF16),
            jax.ShapeDtypeStruct((256, 256), F32),
            jax.ShapeDtypeStruct((1, 512), F32),
        ),
        in_specs=[vmem, vmem, vmem, vmem, vmem, smem, vmem],
        out_specs=(vmem, vmem, vmem, vmem),
        scratch_shapes=[
            buf((2, 32, 64, 512), BF16),
            buf((32, 64, 512), BF16),
            buf((5, 32, 128), F32),
            buf((10, 32, 128), F32),
            buf((128, 128), F32),
            buf((128, 128), F32),
            buf((2, 1, 512), F32),
            buf((2, 1, 512), F32),
            buf((2, 2, 2, 4, 4, 64, 128), BF16),
            buf((2, 8, 4, 64, 128), BF16),
            buf((2, 2, 272, 512), F32),
            buf((2, 2, 272, 512), F32),
            buf((2, 256, 512), BF16),
            buf((2, 256, 512), BF16),
            buf((256, 512), F32),
            buf((2, 2, 256, 512), BF16),
            buf((2, 2, 4, 4, 64, 128), F32),
            buf((2, 2, 2, 4, 4, 64, 128), BF16),
            buf((2, 2, 6, 2, 2, 64, 128), BF16),
            buf((2, 2, 2, 2, 2, 64, 128), BF16),
            buf((2, 4, 2, 64, 128), F32),
            buf((2, 2, 4, 2, 64, 128), BF16),
            buf((2, 2, 3, 2, 64, 128), BF16),
            buf((2, 2, 2, 64, 128), F32),
            buf((2, 2, 4, 64, 128), F32),
            buf((64, 256), BF16),
            buf((64, 256), BF16),
            buf((64, 256), BF16),
            buf((64, 256), BF16),
            buf((256, 256), BF16),
            buf((4, 4, 8, 256), F32),
            buf((3, 4, 8, 256), F32),
            buf((4, 8, 256), F32),
            buf((3, 8, 256), F32),
            buf((4, 8, 256), F32),
            buf((4, 4, 8, 256), F32),
            buf((4, 4, 8, 256), F32),
            pltpu.SemaphoreType.DMA((N_SEM,)),
            pltpu.SemaphoreType.DMA((N_SEM,)),
        ],
        compiler_params=pltpu.CompilerParams(
            collective_id=0, has_side_effects=True, vmem_limit_bytes=48 * 1024 * 1024
        ),
    )(
        features, theta, section_weight.reshape(1, -1), pair_rows, pair_cols, pair_counts, cotangent
    )
    return outs[0], outs[1], outs[2], outs[3].reshape(-1)


def solution(mesh):
    placed = (
        P("ent", None),
        P(),
        P(("ent", "sec")),
        P(("ent", "sec"), None, None),
        P(("ent", "sec"), None, None),
        P(("ent", "sec"), None),
        P("ent", None),
    )
    return jax.shard_map(
        body,
        mesh=mesh,
        in_specs=placed,
        out_specs=(P("ent", None), P("ent", None), P(), P(("ent", "sec"))),
        check_vma=False,
    )
```

```python
import jax
import jax.numpy as jnp
from jax import lax
from jax.experimental import pallas as pl
from jax.experimental.pallas import tpu as pltpu
from jax.sharding import PartitionSpec as P

F32 = jnp.float32
BF16 = jnp.bfloat16
MESH = pl.DeviceIdType.MESH
NT = (((1,), (1,)), ((), ()))
NN = (((1,), (0,)), ((), ()))
N_SEM = 200


def dot(a, b, dims):
    return lax.dot_general(a, b, dims, preferred_element_type=F32)


def split(v):
    hi = v.astype(BF16)
    return hi, (v - hi.astype(F32)).astype(BF16)


def layer(
    feat_h, theta_h, sw_h, rows_h, cols_h, counts_h, cot_h,
    act_o, gf_o, gt_o, gw_o,
    feat, theta, rows, cols, counts, cot,
    HT, HS, DS, DR, D1, DX, D2, DP, DW, DT, SW, INV, XF, XT, G, GR, GH, GL, GATH, MT, PF, PB,
    RB, ACC, YS, YR, A2, XR, AS, AR, FS, FR, TH,
    T0, TP, TX, T3, TS, ssem, rsem, lsem,
):
    e = lax.axis_index("ent")
    s = lax.axis_index("sec")
    core = lax.rem(s, 2)
    xl = lax.div(s, 2)
    xh = lax.div(e, 16)
    z = lax.rem(lax.div(e, 4), 4)
    y = lax.rem(e, 4)
    myx = xh * 2 + xl
    half = pl.multiple_of(core * 64, 64)
    other_half = pl.multiple_of((1 - core) * 64, 64)

    loads = [
        pltpu.make_async_copy(src, dst, lsem.at[i])
        for i, (src, dst) in enumerate([
            (feat_h, feat), (cols_h.at[0], cols), (counts_h, counts), (rows_h.at[0], rows),
            (sw_h, SW.at[0]), (theta_h, theta), (cot_h, cot),
        ])
    ]
    for copy in loads:
        copy.start()

    def dev(xh_, xl_, z_, y_):
        return (xh_ * 16 + z_ * 4 + y_, xl_ * 2 + core)

    def mod4(v):
        return lax.rem(v + 4, 4)

    sib = (e, xl * 2 + 1 - core)
    x_pair = dev(1 - xh, 1 - xl, z, y)
    x_far = dev(1 - xh, xl, z, y)
    x_same = dev(xh, 1 - xl, z, y)

    def z_dev(d):
        return dev(xh, xl, mod4(z + d), y)

    def y_dev(d):
        return dev(xh, xl, z, mod4(y + d))

    plane = [(a, b) for a in range(4) for b in range(4) if a or b]
    plane_dev = [dev(xh, xl, mod4(z + a), mod4(y + b)) for a, b in plane]
    pair_z = [dev(1 - xh, 1 - xl, mod4(z + d), y) for d in range(4)]
    pair_y = [dev(1 - xh, 1 - xl, z, mod4(y + d)) for d in range(4)]
    peers = [sib, x_pair, x_far, x_same] + plane_dev + pair_z[1:] + pair_y[1:]
    sent = []

    def send(src, dst, device):
        i = len(sent)
        copy = pltpu.make_async_remote_copy(
            src_ref=src, dst_ref=dst, send_sem=ssem.at[i], recv_sem=rsem.at[i],
            device_id=device, device_id_type=MESH,
        )
        copy.start()
        sent.append(copy)
        return copy

    def arrived(copies):
        for copy in copies:
            copy.wait_recv()

    barrier = pltpu.get_barrier_semaphore()
    for peer in peers:
        pl.semaphore_signal(barrier, inc=1, device_id=peer, device_id_type=MESH)

    slot_row = lax.broadcasted_iota(jnp.int32, (1, 512), 1)
    ent_iota = lax.broadcasted_iota(jnp.int32, (128, 512), 0)

    def col_table(j):
        live = slot_row < counts[0, j]
        col = jnp.where(live, cols[pl.ds(j, 1), :], -1)
        return jnp.where(ent_iota == col, 1.0, 0.0).astype(BF16)

    loads[0].wait()
    for p in range(2):
        XF[0, p, xh, z, y] = feat[pl.ds(pl.multiple_of(half + 32 * p, 32), 32), :]

    pl.semaphore_wait(barrier, len(peers))

    def all_gather(ph, p, lines=None):
        buf = XF.at[ph, p]
        near_dev, pair_dev, ring_dev = (y_dev, pair_y, z_dev) if p == 0 else (z_dev, pair_z, y_dev)

        def line(a):
            return buf.at[a, z] if p == 0 else buf.at[a, :, y]

        own = buf.at[xh, z, y]
        same = [send(own, own, near_dev(d)) for d in (1, 3, 2)]
        pair = [send(own, own, pair_dev[d]) for d in (0, 1, 3, 2)]
        yield
        arrived(same)
        first = [send(line(xh), line(xh), ring_dev(d)) for d in (1, 3, 2)]
        yield
        arrived(pair)
        second = [send(line(1 - xh), line(1 - xh), ring_dev(d)) for d in (1, 3, 2)]
        yield
        for i in range(3):
            arrived([first[i], second[i]])
            yield

    def degree_sum():
        m = [send(DS, DR, sib)]
        yield
        arrived(m)
        v = DS[...] + DR[...]
        v = jnp.where(core == 0, v[:, 0:64], v[:, 64:128])
        D1[...] = jnp.concatenate([v[0:16], v[16:32]], axis=1)
        m = [send(D1, DX.at[i], d) for i, d in enumerate((x_pair, x_same, x_far))]
        yield
        arrived(m)
        D2[...] = D1[...] + DX[0] + DX[1] + DX[2]
        m = [send(D2, DP.at[i], d) for i, d in enumerate(plane_dev)]
        yield
        arrived(m)
        v = D2[...]
        for i in range(15):
            v = v + DP[i]
        DW[...] = jnp.zeros((128, 128), F32)
        DW[0:16, :] = lax.rsqrt(1.0 + v)
        DT[...] = DW[...].T
        yield

    def step(gens):
        for g in gens:
            next(g, None)

    gathers = [all_gather(0, 0), all_gather(0, 1)]
    step(gathers)
    for copy in loads[1:5]:
        copy.wait()
    ones = jnp.ones((8, 512), BF16)

    def degree_block(j, carry):
        DS[pl.ds(j, 1), :] = dot(ones, col_table(j), NT)[0:1]
        return carry

    lax.fori_loop(0, 32, degree_block, 0)
    degrees = degree_sum()
    step([degrees])
    sw_copy = send(SW.at[0], SW.at[1], sib)

    sec_iota = lax.broadcasted_iota(jnp.int32, (512, 512), 0)

    table_copies = []

    def table_line(k):
        a, b = k // 4, k % 4

        def table_block(i, carry):
            j = 4 * k + i
            row_hot = jnp.where(sec_iota == rows[pl.ds(j, 1), :], 1.0, 0.0).astype(BF16)
            block = dot(col_table(j), row_hot, NT).astype(BF16)
            for h in range(2):
                for p in range(2):
                    HT[h, p, a, b, i] = block[h * 64 + p * 32:h * 64 + p * 32 + 32]
            return carry

        lax.fori_loop(0, 4, table_block, 0)
        table_copies.append(send(HT.at[1 - core, :, a, b], HS.at[:, a, b], sib))

    table_line(0)
    step([degrees])
    table_line(1)
    step(gathers)
    table_line(2)
    step(gathers)
    table_line(3)
    step([degrees])
    for k in range(4, 8):
        table_line(k)
    for copy in loads[5:]:
        copy.wait()
    TH[...] = theta[...].T
    for _ in range(3):
        step(gathers)
    arrived(table_copies)
    arrived([sw_copy])
    step([degrees])
    cols_of = [DT[0:64, 0:16], DT[64:128, 0:16]]

    def scale_of(j, p):
        return cols_of[j // 16][p * 32:p * 32 + 32, j % 16:j % 16 + 1]

    own_table = jnp.where(xh == 0, cols_of[0], cols_of[1])
    own_lane = lax.broadcasted_iota(jnp.int32, (64, 16), 1) == z * 4 + y
    own_scale = jnp.sum(jnp.where(own_lane, own_table, 0.0), axis=1, keepdims=True)

    def table_rows(p, i, k):
        ref = HT.at[core, p] if k == 0 else HS.at[p]
        pieces = [(ref[a, i] if p == 0 else ref[a, :, i]).reshape(128, 512) for a in range(2)]
        return jnp.concatenate(pieces, axis=0)

    def core_sum(ph, k, width):
        return send(G.at[ph, k, 0:width], GR.at[ph, k, 0:width], sib)

    def scaled_line(p, i):
        pieces = []
        for a in range(2):
            for o in range(4):
                b, c = (i, o) if p == 0 else (o, i)
                v = XF[0, p, a, b, c].astype(F32) * scale_of(a * 16 + b * 4 + c, p)
                pieces.append(v.astype(BF16))
        return jnp.concatenate(pieces, axis=0)

    for p in range(2):
        for i in range(4):
            XT[p, i, 0:256] = scaled_line(p, i).T
            XT[p, i, 256:272] = jnp.ones((16, 256), BF16)

    exchange = {}
    for k in (1, 0):
        for p in range(2):

            def gather_line(i, carry):
                v = dot(XT[p, i], table_rows(p, i, k), NN)
                G[0, k] += v
                return carry

            if p == 0:
                G[0, k] = jnp.zeros((272, 512), F32)
            lax.fori_loop(0, 4, gather_line, 0)
        exchange[k] = core_sum(0, k, 272)
    for k in (0, 1):
        arrived([exchange[1 - k]])
        g = G[0, k] + GR[0, 1 - k]
        inverse = 1.0 / (1.0 + g[256:257])
        INV[k] = inverse
        hi, lo = split(g[0:256])
        GH[k] = hi
        GL[k] = lo
        gathered = dot(TH[...], hi, NN) + dot(TH[...], lo, NN)
        if k == 0:
            GATH[...] = gathered
        MT[0, k] = ((SW[k] * inverse) * gathered).astype(BF16)

    def reduce_scatter(ph, out):
        rings = [(z_dev, y_dev, z, y), (y_dev, z_dev, y, z)]

        def term(p, i):
            return dot(table_rows(p, i, 0), MT[ph, 0], NT) + dot(table_rows(p, i, 1), MT[ph, 1], NT)

        ring_copies = [[], []]
        for m, d in enumerate((2, 1, 3)):
            for p in range(2):
                ring_dev, _, ring, _ = rings[p]
                PB[ph, p, m] = term(p, mod4(ring + d)).astype(BF16).reshape(2, 4, 32, 256)
                ring_copies[p].append(send(PB.at[ph, p, m], RB.at[ph, p, m], ring_dev(d)))
        for p in range(2):
            PF[p] = term(p, rings[p][2]).reshape(2, 4, 32, 256)
        yield
        axis_copies = [[], []]
        for p in range(2):
            _, axis_dev, _, axis = rings[p]
            arrived(ring_copies[p])
            for o in range(4):
                for a in range(2):
                    v = PF[p, a, o]
                    for m in range(3):
                        v = v + RB[ph, p, m, a, o].astype(F32)
                    ACC[p, o, a] = v
                    YS[ph, p, o, a] = v.astype(BF16)
            for d in (2, 1, 3):
                axis_copies[p].append(send(YS.at[ph, p, mod4(axis + d)], YR.at[ph, p, d - 1], axis_dev(d)))
        yield
        x_copies = [[], []]
        for p in range(2):
            axis = rings[p][3]
            arrived(axis_copies[p])
            for a in range(2):
                v = ACC[p, axis, a]
                for i in range(3):
                    v = v + YR[ph, p, i, a].astype(F32)
                A2[ph, p, a] = v
            x_copies[p] = [
                send(A2.at[ph, p, 1 - xh], XR.at[ph, p, myx], x_far),
                send(A2.at[ph, p, 1 - xh], XR.at[ph, p, myx], x_pair),
                send(A2.at[ph, p, xh], XR.at[ph, p, myx], x_same),
            ]
            XR[ph, p, myx] = A2[ph, p, xh]
        yield
        for p in range(2):
            arrived(x_copies[p])
            out[p] = (XR[ph, p, 0] + XR[ph, p, 1]) + (XR[ph, p, 2] + XR[ph, p, 3])
            yield

    collected = {}
    flow = reduce_scatter(0, collected)
    for _ in range(3):
        next(flow)
    back = []
    for p in range(2):
        next(flow)
        part = slice(p * 32, p * 32 + 32)
        preact = own_scale[part] * collected[p]
        sig = 1.0 / (1.0 + jnp.exp(-preact))
        AS[part, :] = (preact * sig).astype(BF16)
        upstream = cot[pl.ds(pl.multiple_of(half + p * 32, 32), 32), :].astype(F32)
        grad = upstream * sig * (1.0 + preact * (1.0 - sig))
        XF[1, p, xh, z, y] = (own_scale[part] * grad).astype(BF16)
        back.append(all_gather(1, p))
        step([back[p]])
    act_copy = send(AS, AR, sib)
    for k in range(2):
        G[1, k, 0:256] = jnp.zeros((256, 512), F32)

    def back_line(p, i):
        pieces = [(XF[1, p, a, i] if p == 0 else XF[1, p, a, :, i]).reshape(128, 256) for a in range(2)]
        return jnp.concatenate(pieces, axis=0).T

    step(back)
    step(back)
    for k in range(2):
        G[1, k, 0:256] += dot(back_line(0, z), table_rows(0, z, k), NN)
        G[1, k, 0:256] += dot(back_line(1, y), table_rows(1, y, k), NN)
    act_o[pl.ds(half, 64), :] = AS[...]
    arrived([act_copy])
    act_o[pl.ds(other_half, 64), :] = AR[...]
    for d in (3, 1):
        step(back)
        for p, i in enumerate((mod4(z + d), mod4(y + d))):
            xt = back_line(p, i)
            for k in range(2):
                G[1, k, 0:256] += dot(xt, table_rows(p, i, k), NN)
    step(back)
    last = [(0, mod4(z + 2)), (1, mod4(y + 2))]
    last_xt = [back_line(p, i) for p, i in last]
    for k in (1, 0):
        v = G[1, k, 0:256]
        for (p, i), xt in zip(last, last_xt):
            v = v + dot(xt, table_rows(p, i, k), NN)
        G[1, k, 0:256] = v
        exchange[k] = core_sum(1, k, 256)
    for k in (0, 1):
        arrived([exchange[1 - k]])
        g = G[1, k, 0:256] + GR[1, 1 - k, 0:256]
        if k == 0:
            gw_o[...] = jnp.sum(GATH[...] * g, axis=0, keepdims=True) * INV[0]
        MT[1, k] = ((SW[k] * INV[k]) * g).astype(BF16)

    mine = pl.ds(pl.multiple_of(core * 128, 128), 128)
    theirs = pl.ds(pl.multiple_of((1 - core) * 128, 128), 128)
    v = jnp.zeros((128, 256), F32)
    for k in range(2):
        v = v + dot(GH[k, mine, :], MT[1, k], NT) + dot(GL[k, mine, :], MT[1, k], NT)
    T0[...] = v.reshape(4, 4, 8, 256)
    theta_copies = [
        send(T0.at[mod4(z + a), mod4(y + b)], TP.at[i], plane_dev[i]) for i, (a, b) in enumerate(plane)
    ]
    collected = {}
    flow = reduce_scatter(1, collected)
    next(flow)
    arrived(theta_copies)
    v = T0[z, y]
    for i in range(15):
        v = v + TP[i]
    TX[myx] = v
    theta_copies = [send(TX.at[myx], TX.at[myx], d) for d in (x_far, x_pair, x_same)]
    next(flow)
    arrived(theta_copies)
    T3[z, y] = (TX[0] + TX[1]) + (TX[2] + TX[3])
    theta_copies = [send(T3.at[z, y], T3.at[z, y], d) for d in plane_dev]
    next(flow)
    arrived(theta_copies)
    theta_copies = [send(T3, TS, sib)]
    gt_o[mine, :] = T3[...].reshape(128, 256)
    arrived(theta_copies)
    gt_o[theirs, :] = TS[...].reshape(128, 256)
    for p in range(2):
        next(flow)
        part = slice(p * 32, p * 32 + 32)
        hi, lo = split(own_scale[part] * collected[p])
        FS[part, :] = (dot(hi, theta[...], NT) + dot(lo, theta[...], NT)).astype(BF16)
    grad_copy = send(FS, FR, sib)
    gf_o[pl.ds(half, 64), :] = FS[...]
    arrived([grad_copy])
    gf_o[pl.ds(other_half, 64), :] = FR[...]
    assert len(sent) <= N_SEM
    for copy in sent:
        copy.wait_send()


def body(features, theta, section_weight, pair_rows, pair_cols, pair_counts, cotangent):
    vmem = pl.BlockSpec(memory_space=pltpu.VMEM)
    hbm = pl.BlockSpec(memory_space=pltpu.HBM)

    def buf(shape, dtype):
        return pltpu.VMEM(shape, dtype)

    outs = pl.pallas_call(
        layer,
        out_shape=(
            jax.ShapeDtypeStruct((128, 256), BF16),
            jax.ShapeDtypeStruct((128, 256), BF16),
            jax.ShapeDtypeStruct((256, 256), F32),
            jax.ShapeDtypeStruct((1, 512), F32),
        ),
        in_specs=[hbm] * 7,
        out_specs=(vmem, vmem, vmem, vmem),
        scratch_shapes=[
            buf((128, 256), BF16),
            buf((256, 256), BF16),
            buf((32, 512), jnp.int32),
            buf((32, 512), jnp.int32),
            pltpu.SMEM((1, 32), jnp.int32),
            buf((128, 256), BF16),
            buf((2, 2, 2, 4, 4, 32, 512), BF16),
            buf((2, 2, 4, 4, 32, 512), BF16),
            buf((32, 128), F32),
            buf((32, 128), F32),
            buf((16, 128), F32),
            buf((3, 16, 128), F32),
            buf((16, 128), F32),
            buf((15, 16, 128), F32),
            buf((128, 128), F32),
            buf((128, 128), F32),
            buf((2, 1, 512), F32),
            buf((2, 1, 512), F32),
            buf((2, 2, 2, 4, 4, 32, 256), BF16),
            buf((2, 4, 272, 256), BF16),
            buf((2, 2, 272, 512), F32),
            buf((2, 2, 272, 512), F32),
            buf((2, 256, 512), BF16),
            buf((2, 256, 512), BF16),
            buf((256, 512), F32),
            buf((2, 2, 256, 512), BF16),
            buf((2, 2, 4, 32, 256), F32),
            buf((2, 2, 3, 2, 4, 32, 256), BF16),
            buf((2, 2, 3, 2, 4, 32, 256), BF16),
            buf((2, 4, 2, 32, 256), F32),
            buf((2, 2, 4, 2, 32, 256), BF16),
            buf((2, 2, 3, 2, 32, 256), BF16),
            buf((2, 2, 2, 32, 256), F32),
            buf((2, 2, 4, 32, 256), F32),
            buf((64, 256), BF16),
            buf((64, 256), BF16),
            buf((64, 256), BF16),
            buf((64, 256), BF16),
            buf((256, 256), BF16),
            buf((4, 4, 8, 256), F32),
            buf((15, 8, 256), F32),
            buf((4, 8, 256), F32),
            buf((4, 4, 8, 256), F32),
            buf((4, 4, 8, 256), F32),
            pltpu.SemaphoreType.DMA((N_SEM,)),
            pltpu.SemaphoreType.DMA((N_SEM,)),
            pltpu.SemaphoreType.DMA((7,)),
        ],
        compiler_params=pltpu.CompilerParams(
            collective_id=0, has_side_effects=True, vmem_limit_bytes=56 * 1024 * 1024
        ),
    )(
        features, theta, section_weight.reshape(1, -1), pair_rows, pair_cols, pair_counts, cotangent
    )
    return outs[0], outs[1], outs[2], outs[3].reshape(-1)


def solution(mesh):
    placed = (
        P("ent", None),
        P(),
        P(("ent", "sec")),
        P(("ent", "sec"), None, None),
        P(("ent", "sec"), None, None),
        P(("ent", "sec"), None),
        P("ent", None),
    )
    return jax.shard_map(
        body,
        mesh=mesh,
        in_specs=placed,
        out_specs=(P("ent", None), P("ent", None), P(), P(("ent", "sec"))),
        check_vma=False,
    )
```

```python
import jax
import jax.numpy as jnp
from jax import lax
from jax.experimental import pallas as pl
from jax.experimental.pallas import tpu as pltpu
from jax.sharding import PartitionSpec as P

F32 = jnp.float32
BF16 = jnp.bfloat16
MESH = pl.DeviceIdType.MESH
NT = (((1,), (1,)), ((), ()))
NN = (((1,), (0,)), ((), ()))
N_SEM = 200


def dot(a, b, dims):
    return lax.dot_general(a, b, dims, preferred_element_type=F32)


def split(v):
    hi = v.astype(BF16)
    return hi, (v - hi.astype(F32)).astype(BF16)


def layer(
    feat_h, theta_h, sw_h, rows_h, cols_h, counts_h, cot_h,
    act_o, gf_o, gt_o, gw_o,
    feat, theta, rows, cols, counts, cot,
    HT, HS, DS, DR, D1, DX, D2, DP, DW, DT, SW, INV, XF, SC, G, GR, GH, GL, GATH, MT, PF, PB,
    RB, ACC, YS, YR, A2, XR, AS, AR, FS, FR, TH,
    T0, TP, TX, T3, TS, ssem, rsem, lsem,
):
    e = lax.axis_index("ent")
    s = lax.axis_index("sec")
    core = lax.rem(s, 2)
    xl = lax.div(s, 2)
    xh = lax.div(e, 16)
    z = lax.rem(lax.div(e, 4), 4)
    y = lax.rem(e, 4)
    myx = xh * 2 + xl
    half = pl.multiple_of(core * 64, 64)
    other_half = pl.multiple_of((1 - core) * 64, 64)

    loads = [
        pltpu.make_async_copy(src, dst, lsem.at[i])
        for i, (src, dst) in enumerate([
            (feat_h, feat), (cols_h.at[0], cols), (counts_h, counts), (rows_h.at[0], rows),
            (sw_h, SW.at[0]), (theta_h, theta), (cot_h, cot),
        ])
    ]
    for copy in loads:
        copy.start()

    def dev(xh_, xl_, z_, y_):
        return (xh_ * 16 + z_ * 4 + y_, xl_ * 2 + core)

    def mod4(v):
        return lax.rem(v + 4, 4)

    sib = (e, xl * 2 + 1 - core)
    x_pair = dev(1 - xh, 1 - xl, z, y)
    x_far = dev(1 - xh, xl, z, y)
    x_same = dev(xh, 1 - xl, z, y)

    def z_dev(d):
        return dev(xh, xl, mod4(z + d), y)

    def y_dev(d):
        return dev(xh, xl, z, mod4(y + d))

    plane = [(a, b) for a in range(4) for b in range(4) if a or b]
    plane_dev = [dev(xh, xl, mod4(z + a), mod4(y + b)) for a, b in plane]
    pair_z = [dev(1 - xh, 1 - xl, mod4(z + d), y) for d in range(4)]
    pair_y = [dev(1 - xh, 1 - xl, z, mod4(y + d)) for d in range(4)]
    peers = [sib, x_pair, x_far, x_same] + plane_dev + pair_z[1:] + pair_y[1:]
    sent = []

    def send(src, dst, device):
        i = len(sent)
        copy = pltpu.make_async_remote_copy(
            src_ref=src, dst_ref=dst, send_sem=ssem.at[i], recv_sem=rsem.at[i],
            device_id=device, device_id_type=MESH,
        )
        copy.start()
        sent.append(copy)
        return copy

    def arrived(copies):
        for copy in copies:
            copy.wait_recv()

    barrier = pltpu.get_barrier_semaphore()
    for peer in peers:
        pl.semaphore_signal(barrier, inc=1, device_id=peer, device_id_type=MESH)

    slot_row = lax.broadcasted_iota(jnp.int32, (1, 512), 1)
    ent_iota = lax.broadcasted_iota(jnp.int32, (128, 512), 0)

    def col_table(j):
        live = slot_row < counts[0, j]
        col = jnp.where(live, cols[pl.ds(j, 1), :], -1)
        return jnp.where(ent_iota == col, 1.0, 0.0).astype(BF16)

    for copy in loads[1:3]:
        copy.wait()
    ones = jnp.ones((8, 512), BF16)
    for k in range(8):
        table = jnp.concatenate([col_table(4 * k + i) for i in range(4)], axis=0)
        DS[k:k + 1, :] = dot(ones, table, NT)[0:1]

    loads[0].wait()
    for p in range(2):
        XF[0, p, xh, z, y] = feat[pl.ds(pl.multiple_of(half + 32 * p, 32), 32), :]

    pl.semaphore_wait(barrier, len(peers))

    def all_gather(ph, p, lines=None):
        buf = XF.at[ph, p]
        near_dev, pair_dev, ring_dev = (y_dev, pair_y, z_dev) if p == 0 else (z_dev, pair_z, y_dev)

        def line(a):
            return buf.at[a, z] if p == 0 else buf.at[a, :, y]

        own = buf.at[xh, z, y]
        same = [send(own, own, near_dev(d)) for d in (1, 3, 2)]
        pair = [send(own, own, pair_dev[d]) for d in (0, 1, 3, 2)]
        yield
        arrived(same)
        first = [send(line(xh), line(xh), ring_dev(d)) for d in (1, 3, 2)]
        yield
        arrived(pair)
        second = [send(line(1 - xh), line(1 - xh), ring_dev(d)) for d in (1, 3, 2)]
        yield
        for i in range(3):
            arrived([first[i], second[i]])
            yield

    def degree_sum():
        m = [send(DS, DR, sib)]
        yield
        arrived(m)
        v = DS[...] + DR[...]
        v = jnp.concatenate([v[:, i * 128:(i + 1) * 128] for i in range(4)], axis=0)
        v = jnp.where(core == 0, v[:, 0:64], v[:, 64:128])
        D1[...] = jnp.concatenate([v[0:16], v[16:32]], axis=1)
        m = [send(D1, DX.at[i], d) for i, d in enumerate((x_pair, x_same, x_far))]
        yield
        arrived(m)
        D2[...] = D1[...] + DX[0] + DX[1] + DX[2]
        m = [send(D2, DP.at[i], d) for i, d in enumerate(plane_dev)]
        yield
        arrived(m)
        v = D2[...]
        for i in range(15):
            v = v + DP[i]
        DW[...] = jnp.zeros((128, 128), F32)
        DW[0:16, :] = lax.rsqrt(1.0 + v)
        DT[...] = DW[...].T
        yield

    def step(gens):
        for g in gens:
            next(g, None)

    degrees = degree_sum()
    step([degrees])
    gathers = [all_gather(0, 0), all_gather(0, 1)]
    step(gathers)
    loads[3].wait()

    sec_iota = lax.broadcasted_iota(jnp.int32, (512, 512), 0)

    table_copies = []

    def table_line(k):
        a, b = k // 4, k % 4

        def table_block(i, carry):
            j = 4 * k + i
            row_hot = jnp.where(sec_iota == rows[pl.ds(j, 1), :], 1.0, 0.0).astype(BF16)
            block = dot(col_table(j), row_hot, NT).astype(BF16)
            for h in range(2):
                for p in range(2):
                    HT[h, p, a, b, i] = block[h * 64 + p * 32:h * 64 + p * 32 + 32]
            return carry

        lax.fori_loop(0, 4, table_block, 0)
        table_copies.append(send(HT.at[1 - core, :, a, b], HS.at[:, a, b], sib))

    step([degrees])
    for k in range(3):
        table_line(k)
    step([degrees])
    step(gathers)
    step(gathers)
    loads[4].wait()
    sw_copy = send(SW.at[0], SW.at[1], sib)
    for k in range(3, 8):
        table_line(k)
    for copy in loads[5:]:
        copy.wait()
    TH[...] = theta[...].T
    step([degrees])
    cols_of = [DT[0:64, 0:16], DT[64:128, 0:16]]
    for c in range(4):
        for a in range(2):
            for b in range(4):
                r = c * 8 + a * 4 + b
                column = cols_of[r // 16][:, r % 16:r % 16 + 1]
                for p in range(2):
                    SC[p, a, b, c] = jnp.broadcast_to(column[p * 32:p * 32 + 32], (32, 128))

    own_scale = jnp.concatenate([SC[p, xh, z, y] for p in range(2)], axis=0)
    own_scale = jnp.concatenate([own_scale, own_scale], axis=1)

    def table_rows(p, i, k):
        ref = HT.at[core, p] if k == 0 else HS.at[p]
        pieces = [(ref[a, i] if p == 0 else ref[a, :, i]).reshape(128, 512) for a in range(2)]
        return jnp.concatenate(pieces, axis=0)

    def core_sum(ph, k, width):
        return send(G.at[ph, k, 0:width], GR.at[ph, k, 0:width], sib)

    def line_of(ref, p, a, i):
        return ref[p, a, i] if p == 0 else ref[p, a, :, i]

    def gather_line(ph, p, i):
        pieces = []
        for a in range(2):
            v = line_of(XF.at[ph], p, a, i).reshape(128, 256)
            if ph == 0:
                scale = line_of(SC, p, a, i).reshape(128, 128)
                v = (v.astype(F32) * jnp.concatenate([scale, scale], axis=1)).astype(BF16)
            pieces.append(v)
        xt = jnp.concatenate(pieces, axis=0).T
        if ph == 0:
            xt = jnp.concatenate([xt, jnp.ones((16, 256), BF16)], axis=0)
        return xt

    def gather_sections(ph, gathers):
        width = 272 if ph == 0 else 256
        exchange = {}
        for k in range(2):
            v = None
            for p, i in enumerate((z, y)):
                t = dot(gather_line(ph, p, i), table_rows(p, i, k), NN)
                v = t if v is None else v + t
            G[ph, k, 0:width] = v
        for d in (3, 1):
            step(gathers)
            for p, i in enumerate((mod4(z + d), mod4(y + d))):
                xt = gather_line(ph, p, i)
                for k in range(2):
                    G[ph, k, 0:width] += dot(xt, table_rows(p, i, k), NN)
        step(gathers)
        last = [(0, mod4(z + 2)), (1, mod4(y + 2))]
        xts = [gather_line(ph, p, i) for p, i in last]
        for k in (1, 0):
            v = G[ph, k, 0:width]
            for (p, i), xt in zip(last, xts):
                v = v + dot(xt, table_rows(p, i, k), NN)
            G[ph, k, 0:width] = v
            exchange[k] = core_sum(ph, k, width)
        return exchange

    arrived(table_copies)
    arrived([sw_copy])
    exchange = gather_sections(0, gathers)
    for k in (0, 1):
        arrived([exchange[1 - k]])
        g = G[0, k] + GR[0, 1 - k]
        inverse = 1.0 / (1.0 + g[256:257])
        INV[k] = inverse
        hi, lo = split(g[0:256])
        GH[k] = hi
        GL[k] = lo
        gathered = dot(TH[...], hi, NN) + dot(TH[...], lo, NN)
        if k == 0:
            GATH[...] = gathered
        MT[0, k] = ((SW[k] * inverse) * gathered).astype(BF16)

    def reduce_scatter(ph, out):
        rings = [(z_dev, y_dev, z, y), (y_dev, z_dev, y, z)]

        def term(p, i):
            return dot(table_rows(p, i, 0), MT[ph, 0], NT) + dot(table_rows(p, i, 1), MT[ph, 1], NT)

        ring_copies = [[], []]
        for m, d in enumerate((2, 1, 3)):
            for p in range(2):
                ring_dev, _, ring, _ = rings[p]
                PB[ph, p, m] = term(p, mod4(ring + d)).astype(BF16).reshape(2, 4, 32, 256)
                ring_copies[p].append(send(PB.at[ph, p, m], RB.at[ph, p, m], ring_dev(d)))
        for p in range(2):
            PF[p] = term(p, rings[p][2]).reshape(2, 4, 32, 256)
        yield
        axis_copies = [[], []]
        for p in range(2):
            _, axis_dev, _, axis = rings[p]
            arrived(ring_copies[p])
            for o in range(4):
                for a in range(2):
                    v = PF[p, a, o]
                    for m in range(3):
                        v = v + RB[ph, p, m, a, o].astype(F32)
                    ACC[p, o, a] = v
                    YS[ph, p, o, a] = v.astype(BF16)
            for d in (2, 1, 3):
                axis_copies[p].append(send(YS.at[ph, p, mod4(axis + d)], YR.at[ph, p, d - 1], axis_dev(d)))
        yield
        x_copies = [[], []]
        for p in range(2):
            axis = rings[p][3]
            arrived(axis_copies[p])
            for a in range(2):
                v = ACC[p, axis, a]
                for i in range(3):
                    v = v + YR[ph, p, i, a].astype(F32)
                A2[ph, p, a] = v.astype(BF16)
            x_copies[p] = [
                send(A2.at[ph, p, 1 - xh], XR.at[ph, p, myx], x_far),
                send(A2.at[ph, p, 1 - xh], XR.at[ph, p, myx], x_pair),
                send(A2.at[ph, p, xh], XR.at[ph, p, myx], x_same),
            ]
            XR[ph, p, myx] = A2[ph, p, xh]
        yield
        for p in range(2):
            arrived(x_copies[p])
            terms = [XR[ph, p, i].astype(F32) for i in range(4)]
            out[p] = (terms[0] + terms[1]) + (terms[2] + terms[3])
            yield

    collected = {}
    flow = reduce_scatter(0, collected)
    next(flow)
    next(flow)
    next(flow)
    back = []
    for p in range(2):
        next(flow)
        part = slice(p * 32, p * 32 + 32)
        preact = own_scale[part] * collected[p]
        sig = 1.0 / (1.0 + jnp.exp(-preact))
        AS[part, :] = (preact * sig).astype(BF16)
        upstream = cot[pl.ds(pl.multiple_of(half + p * 32, 32), 32), :].astype(F32)
        grad = upstream * sig * (1.0 + preact * (1.0 - sig))
        XF[1, p, xh, z, y] = (own_scale[part] * grad).astype(BF16)
        back.append(all_gather(1, p))
        step([back[p]])
    act_copy = send(AS, AR, sib)
    step(back)
    step(back)
    act_o[pl.ds(half, 64), :] = AS[...]
    arrived([act_copy])
    act_o[pl.ds(other_half, 64), :] = AR[...]
    exchange = gather_sections(1, back)
    for k in (0, 1):
        arrived([exchange[1 - k]])
        g = G[1, k, 0:256] + GR[1, 1 - k, 0:256]
        if k == 0:
            gw_o[...] = jnp.sum(GATH[...] * g, axis=0, keepdims=True) * INV[0]
        MT[1, k] = ((SW[k] * INV[k]) * g).astype(BF16)

    mine = pl.ds(pl.multiple_of(core * 128, 128), 128)
    theirs = pl.ds(pl.multiple_of((1 - core) * 128, 128), 128)
    v = jnp.zeros((128, 256), F32)
    for k in range(2):
        v = v + dot(GH[k, mine, :], MT[1, k], NT) + dot(GL[k, mine, :], MT[1, k], NT)
    T0[...] = v.reshape(4, 4, 8, 256)
    theta_copies = [
        send(T0.at[mod4(z + a), mod4(y + b)], TP.at[i], plane_dev[i]) for i, (a, b) in enumerate(plane)
    ]
    collected = {}
    flow = reduce_scatter(1, collected)
    next(flow)
    arrived(theta_copies)
    v = T0[z, y]
    for i in range(15):
        v = v + TP[i]
    TX[myx] = v
    theta_copies = [send(TX.at[myx], TX.at[myx], d) for d in (x_far, x_pair, x_same)]
    next(flow)
    arrived(theta_copies)
    T3[z, y] = (TX[0] + TX[1]) + (TX[2] + TX[3])
    theta_copies = [send(T3.at[z, y], T3.at[z, y], d) for d in plane_dev]
    next(flow)
    arrived(theta_copies)
    theta_copies = [send(T3, TS, sib)]
    gt_o[mine, :] = T3[...].reshape(128, 256)
    arrived(theta_copies)
    gt_o[theirs, :] = TS[...].reshape(128, 256)
    for p in range(2):
        next(flow)
        part = slice(p * 32, p * 32 + 32)
        hi, lo = split(own_scale[part] * collected[p])
        FS[part, :] = (dot(hi, theta[...], NT) + dot(lo, theta[...], NT)).astype(BF16)
    grad_copy = send(FS, FR, sib)
    gf_o[pl.ds(half, 64), :] = FS[...]
    arrived([grad_copy])
    gf_o[pl.ds(other_half, 64), :] = FR[...]
    assert len(sent) <= N_SEM
    for copy in sent:
        copy.wait_send()


def write_out(a, b, c, d, a_o, b_o, c_o, d_o, sem):
    pairs = [(a, a_o), (b, b_o), (c, c_o), (d, d_o)]
    copies = [pltpu.make_async_copy(src, dst, sem.at[i]) for i, (src, dst) in enumerate(pairs)]
    for copy in copies:
        copy.start()
    for copy in copies:
        copy.wait()


def body(features, theta, section_weight, pair_rows, pair_cols, pair_counts, cotangent):
    vmem = pl.BlockSpec(memory_space=pltpu.VMEM)
    hbm = pl.BlockSpec(memory_space=pltpu.HBM)

    def buf(shape, dtype):
        return pltpu.VMEM(shape, dtype)

    ins = (features, theta, section_weight.reshape(1, -1), pair_rows, pair_cols, pair_counts, cotangent)
    ins = [pltpu.with_memory_space_constraint(v, pltpu.HBM) for v in ins]
    outs = pl.pallas_call(
        layer,
        out_shape=(
            jax.ShapeDtypeStruct((128, 256), BF16),
            jax.ShapeDtypeStruct((128, 256), BF16),
            jax.ShapeDtypeStruct((256, 256), F32),
            jax.ShapeDtypeStruct((1, 512), F32),
        ),
        in_specs=[hbm] * 7,
        out_specs=(vmem, vmem, vmem, vmem),
        scratch_shapes=[
            buf((128, 256), BF16),
            buf((256, 256), BF16),
            buf((32, 512), jnp.int32),
            buf((32, 512), jnp.int32),
            pltpu.SMEM((1, 32), jnp.int32),
            buf((128, 256), BF16),
            buf((2, 2, 2, 4, 4, 32, 512), BF16),
            buf((2, 2, 4, 4, 32, 512), BF16),
            buf((8, 512), F32),
            buf((8, 512), F32),
            buf((16, 128), F32),
            buf((3, 16, 128), F32),
            buf((16, 128), F32),
            buf((15, 16, 128), F32),
            buf((128, 128), F32),
            buf((128, 128), F32),
            buf((2, 1, 512), F32),
            buf((2, 1, 512), F32),
            buf((2, 2, 2, 4, 4, 32, 256), BF16),
            buf((2, 2, 4, 4, 32, 128), F32),
            buf((2, 2, 272, 512), F32),
            buf((2, 2, 272, 512), F32),
            buf((2, 256, 512), BF16),
            buf((2, 256, 512), BF16),
            buf((256, 512), F32),
            buf((2, 2, 256, 512), BF16),
            buf((2, 2, 4, 32, 256), F32),
            buf((2, 2, 3, 2, 4, 32, 256), BF16),
            buf((2, 2, 3, 2, 4, 32, 256), BF16),
            buf((2, 4, 2, 32, 256), F32),
            buf((2, 2, 4, 2, 32, 256), BF16),
            buf((2, 2, 3, 2, 32, 256), BF16),
            buf((2, 2, 2, 32, 256), BF16),
            buf((2, 2, 4, 32, 256), BF16),
            buf((64, 256), BF16),
            buf((64, 256), BF16),
            buf((64, 256), BF16),
            buf((64, 256), BF16),
            buf((256, 256), BF16),
            buf((4, 4, 8, 256), F32),
            buf((15, 8, 256), F32),
            buf((4, 8, 256), F32),
            buf((4, 4, 8, 256), F32),
            buf((4, 4, 8, 256), F32),
            pltpu.SemaphoreType.DMA((N_SEM,)),
            pltpu.SemaphoreType.DMA((N_SEM,)),
            pltpu.SemaphoreType.DMA((7,)),
        ],
        compiler_params=pltpu.CompilerParams(
            collective_id=0, has_side_effects=True, vmem_limit_bytes=40 * 1024 * 1024
        ),
    )(*ins)
    anywhere = pl.BlockSpec(memory_space=pl.ANY)
    outs = pl.pallas_call(
        write_out,
        out_shape=tuple(jax.ShapeDtypeStruct(o.shape, o.dtype) for o in outs),
        in_specs=[vmem] * 4,
        out_specs=(anywhere,) * 4,
        scratch_shapes=[pltpu.SemaphoreType.DMA((4,))],
        compiler_params=pltpu.CompilerParams(vmem_limit_bytes=4 * 1024 * 1024),
    )(*outs)
    return outs[0], outs[1], outs[2], outs[3].reshape(-1)


def solution(mesh):
    placed = (
        P("ent", None),
        P(),
        P(("ent", "sec")),
        P(("ent", "sec"), None, None),
        P(("ent", "sec"), None, None),
        P(("ent", "sec"), None),
        P("ent", None),
    )
    return jax.shard_map(
        body,
        mesh=mesh,
        in_specs=placed,
        out_specs=(P("ent", None), P("ent", None), P(), P(("ent", "sec"))),
        check_vma=False,
    )
```

```python
import jax
import jax.numpy as jnp
from jax import lax
from jax.experimental import pallas as pl
from jax.experimental.pallas import tpu as pltpu
from jax.sharding import PartitionSpec as P

F32 = jnp.float32
BF16 = jnp.bfloat16
F8 = jnp.float8_e4m3fn
MESH = pl.DeviceIdType.MESH
NT = (((1,), (1,)), ((), ()))
NN = (((1,), (0,)), ((), ()))
N_SEM = 48


def dot(a, b, dims):
    return lax.dot_general(a, b, dims, preferred_element_type=F32)


def split(v):
    hi = v.astype(BF16)
    return hi, (v - hi.astype(F32)).astype(BF16)


def layer(
    feat_h, theta_h, sw_h, rows_h, cols_h, counts_h, cot_h,
    act_o, gf_o, gt_o, gw_o,
    feat, theta, rows, cols, counts, cot,
    HT, HS, DS, DR, D1, DX, D2, DP, DW, DT, SW, INV, XF, SC, G, GR, LF, LB, LR, GH, GL, GATH, MT, PF, PB,
    RB, ACC, YS, YR, A2, XR, AS, AR, FS, FR, TH,
    T0, TP, TX, T3, TS, ssem, rsem, lsem,
):
    e = lax.axis_index("ent")
    s = lax.axis_index("sec")
    core = lax.rem(s, 2)
    xl = lax.div(s, 2)
    xh = lax.div(e, 16)
    z = lax.rem(lax.div(e, 4), 4)
    y = lax.rem(e, 4)
    myx = xh * 2 + xl
    half = pl.multiple_of(core * 64, 64)
    other_half = pl.multiple_of((1 - core) * 64, 64)

    loads = [
        pltpu.make_async_copy(src, dst, lsem.at[i])
        for i, (src, dst) in enumerate([
            (feat_h, feat), (cols_h.at[0], cols), (counts_h, counts), (rows_h.at[0], rows),
            (sw_h, SW.at[0]), (theta_h, theta), (cot_h, cot),
        ])
    ]
    for copy in loads:
        copy.start()

    def dev(xh_, xl_, z_, y_):
        return (xh_ * 16 + z_ * 4 + y_, xl_ * 2 + core)

    def mod4(v):
        return lax.rem(v + 4, 4)

    sib = (e, xl * 2 + 1 - core)
    x_pair = dev(1 - xh, 1 - xl, z, y)
    x_far = dev(1 - xh, xl, z, y)
    x_same = dev(xh, 1 - xl, z, y)

    def z_dev(d):
        return dev(xh, xl, mod4(z + d), y)

    def y_dev(d):
        return dev(xh, xl, z, mod4(y + d))

    plane = [(a, b) for a in range(4) for b in range(4) if a or b]
    plane_dev = [dev(xh, xl, mod4(z + a), mod4(y + b)) for a, b in plane]
    pair_z = [dev(1 - xh, 1 - xl, mod4(z + d), y) for d in range(4)]
    pair_y = [dev(1 - xh, 1 - xl, z, mod4(y + d)) for d in range(4)]
    peers = [sib, x_pair, x_far, x_same] + plane_dev + pair_z[1:] + pair_y[1:]
    groups = []

    def open_group(size):
        groups.append(size)
        return len(groups) - 1

    def send(g, src, dst, device):
        pltpu.make_async_remote_copy(
            src_ref=src, dst_ref=dst, send_sem=ssem.at[g], recv_sem=rsem.at[g],
            device_id=device, device_id_type=MESH,
        ).start()

    def whole(g):
        return pltpu.make_async_remote_copy(
            src_ref=groups[g], dst_ref=groups[g], send_sem=ssem.at[g], recv_sem=rsem.at[g],
            device_id=sib, device_id_type=MESH,
        )

    def send_all(size, copies):
        g = open_group(size)
        for src, dst, device in copies:
            send(g, src, dst, device)
        return g

    def arrived(g):
        whole(g).wait_recv()

    barrier = pltpu.get_barrier_semaphore()
    for peer in peers:
        pl.semaphore_signal(barrier, inc=1, device_id=peer, device_id_type=MESH)

    slot_row = lax.broadcasted_iota(jnp.int32, (1, 512), 1)
    ent_iota = lax.broadcasted_iota(jnp.int32, (128, 512), 0)

    def col_table(j):
        live = slot_row < counts[0, j]
        col = jnp.where(live, cols[pl.ds(j, 1), :], -1)
        return jnp.where(ent_iota == col, 1.0, 0.0).astype(F8)

    for copy in loads[1:3]:
        copy.wait()
    ones = jnp.ones((8, 512), F8)
    for k in range(8):
        table = jnp.concatenate([col_table(4 * k + i) for i in range(4)], axis=0)
        DS[k:k + 1, :] = dot(ones, table, NT)[0:1]

    loads[0].wait()
    for p in range(2):
        XF[0, p, xh, z, y] = feat[pl.ds(pl.multiple_of(half + 32 * p, 32), 32), :]

    pl.semaphore_wait(barrier, len(peers))

    def all_gather(ph, p, lines=None):
        buf = XF.at[ph, p]
        near_dev, pair_dev, ring_dev = (y_dev, pair_y, z_dev) if p == 0 else (z_dev, pair_z, y_dev)

        def line(a):
            return buf.at[a, z] if p == 0 else buf.at[a, :, y]

        own = buf.at[xh, z, y]
        same = send_all(buf.at[0, 0, 0:3], [(own, own, near_dev(d)) for d in (1, 3, 2)])
        pair = send_all(buf.at[0, 0], [(own, own, pair_dev[d]) for d in (0, 1, 3, 2)])
        rings = {d: open_group(buf.at[0, 0:2]) for d in (1, 3, 2)}
        yield
        for stage, a in ((same, xh), (pair, 1 - xh)):
            arrived(stage)
            for d in (1, 3, 2):
                send(rings[d], line(a), line(a), ring_dev(d))
            yield
        for d in (1, 3, 2):
            arrived(rings[d])
            yield

    def degree_sum():
        m = send_all(DR, [(DS, DR, sib)])
        yield
        arrived(m)
        v = DS[...] + DR[...]
        v = jnp.concatenate([v[:, i * 128:(i + 1) * 128] for i in range(4)], axis=0)
        v = jnp.where(core == 0, v[:, 0:64], v[:, 64:128])
        D1[...] = jnp.concatenate([v[0:16], v[16:32]], axis=1)
        m = send_all(DX, [(D1, DX.at[i], d) for i, d in enumerate((x_pair, x_same, x_far))])
        yield
        arrived(m)
        D2[...] = D1[...] + DX[0] + DX[1] + DX[2]
        m = send_all(DP, [(D2, DP.at[i], d) for i, d in enumerate(plane_dev)])
        yield
        arrived(m)
        v = D2[...]
        for i in range(15):
            v = v + DP[i]
        DW[...] = jnp.zeros((128, 128), F32)
        DW[0:16, :] = lax.rsqrt(1.0 + v)
        DT[...] = DW[...].T
        yield

    def step(gens):
        for g in gens:
            next(g, None)

    degrees = degree_sum()
    step([degrees])
    gathers = [all_gather(0, 0), all_gather(0, 1)]
    step(gathers)
    loads[3].wait()

    sec_iota = lax.broadcasted_iota(jnp.int32, (512, 512), 0)

    table_group = open_group(HS)

    def table_line(k):
        a, b = k // 4, k % 4

        def table_block(i, carry):
            j = 4 * k + i
            row_hot = jnp.where(sec_iota == rows[pl.ds(j, 1), :], 1.0, 0.0).astype(F8)
            block = dot(col_table(j), row_hot, NT).astype(BF16)
            for h in range(2):
                for p in range(2):
                    HT[h, p, a, b, i] = block[h * 64 + p * 32:h * 64 + p * 32 + 32]
            return carry

        lax.fori_loop(0, 4, table_block, 0)
        send(table_group, HT.at[1 - core, :, a, b], HS.at[:, a, b], sib)

    step([degrees])
    for k in range(3):
        table_line(k)
    step([degrees])
    step(gathers)
    step(gathers)
    loads[4].wait()
    sw_group = send_all(SW.at[1], [(SW.at[0], SW.at[1], sib)])
    for k in range(3, 8):
        table_line(k)
    for copy in loads[5:]:
        copy.wait()
    TH[...] = theta[...].T
    step([degrees])
    cols_of = [DT[0:64, 0:16], DT[64:128, 0:16]]
    for c in range(4):
        for a in range(2):
            for b in range(4):
                r = c * 8 + a * 4 + b
                column = cols_of[r // 16][:, r % 16:r % 16 + 1]
                for p in range(2):
                    SC[p, a, b, c] = jnp.broadcast_to(column[p * 32:p * 32 + 32], (32, 128))

    own_scale = jnp.concatenate([SC[p, xh, z, y] for p in range(2)], axis=0)
    own_scale = jnp.concatenate([own_scale, own_scale], axis=1)

    def table_rows(p, i, k):
        ref = HT.at[core, p] if k == 0 else HS.at[p]
        pieces = [(ref[a, i] if p == 0 else ref[a, :, i]).reshape(128, 512) for a in range(2)]
        return jnp.concatenate(pieces, axis=0)

    def core_sum(src, dst):
        return send_all(dst, [(src, dst, sib)])

    def line_of(ref, p, a, i):
        return ref[p, a, i] if p == 0 else ref[p, a, :, i]

    def gather_line(ph, p, i):
        pieces = []
        for a in range(2):
            v = line_of(XF.at[ph], p, a, i).reshape(128, 256)
            if ph == 0:
                scale = line_of(SC, p, a, i).reshape(128, 128)
                v = (v.astype(F32) * jnp.concatenate([scale, scale], axis=1)).astype(BF16)
            pieces.append(v)
        xt = jnp.concatenate(pieces, axis=0).T
        if ph == 0:
            xt = jnp.concatenate([xt, jnp.ones((16, 256), BF16)], axis=0)
        return xt

    def gather_sections(ph, gathers):
        width = 272 if ph == 0 else 256
        exchange = []
        for k in range(2):
            v = None
            for p, i in enumerate((z, y)):
                t = dot(gather_line(ph, p, i), table_rows(p, i, k), NN)
                v = t if v is None else v + t
            G[ph, k, 0:width] = v
        for d in (3, 1):
            step(gathers)
            for p, i in enumerate((mod4(z + d), mod4(y + d))):
                xt = gather_line(ph, p, i)
                for k in range(2):
                    G[ph, k, 0:width] += dot(xt, table_rows(p, i, k), NN)
        if ph == 1:
            exchange.append(send_all(GR.at[1, :, 0:256], [(G.at[1, :, 0:256], GR.at[1, :, 0:256], sib)]))
        step(gathers)
        last = [(0, mod4(z + 2)), (1, mod4(y + 2))]
        xts = [gather_line(ph, p, i) for p, i in last]
        for k in (1, 0):
            v = None
            for (p, i), xt in zip(last, xts):
                t = dot(xt, table_rows(p, i, k), NN)
                v = t if v is None else v + t
            if ph == 0:
                G[0, k] += v
                exchange.append(core_sum(G.at[0, k], GR.at[0, k]))
            else:
                LF[k] = v
                LB[k] = v.astype(BF16)
                exchange.append(core_sum(LB.at[k], LR.at[k]))
        return exchange

    arrived(table_group)
    arrived(sw_group)
    exchange = gather_sections(0, gathers)
    for k in (0, 1):
        arrived(exchange[k])
        g = G[0, k] + GR[0, 1 - k]
        inverse = 1.0 / (1.0 + g[256:257])
        INV[k] = inverse
        hi, lo = split(g[0:256])
        GH[k] = hi
        GL[k] = lo
        gathered = dot(TH[...], hi, NN) + dot(TH[...], lo, NN)
        if k == 0:
            GATH[...] = gathered
        MT[0, k] = ((SW[k] * inverse) * gathered).astype(BF16)

    def reduce_scatter(ph, out):
        rings = [(z_dev, y_dev, z, y), (y_dev, z_dev, y, z)]

        def term(p, i):
            return dot(table_rows(p, i, 0), MT[ph, 0], NT) + dot(table_rows(p, i, 1), MT[ph, 1], NT)

        ring_groups = [open_group(RB.at[ph, p]) for p in range(2)]
        for m, d in enumerate((2, 1, 3)):
            for p in range(2):
                ring_dev, _, ring, _ = rings[p]
                PB[ph, p, m] = term(p, mod4(ring + d)).astype(BF16).reshape(2, 4, 32, 256)
                send(ring_groups[p], PB.at[ph, p, m], RB.at[ph, p, m], ring_dev(d))
        for p in range(2):
            PF[p] = term(p, rings[p][2]).reshape(2, 4, 32, 256)
        yield
        axis_groups = []
        for p in range(2):
            _, axis_dev, _, axis = rings[p]
            arrived(ring_groups[p])
            for o in range(4):
                for a in range(2):
                    v = PF[p, a, o]
                    for m in range(3):
                        v = v + RB[ph, p, m, a, o].astype(F32)
                    ACC[p, o, a] = v
                    YS[ph, p, o, a] = v.astype(BF16)
            axis_groups.append(send_all(
                YR.at[ph, p],
                [(YS.at[ph, p, mod4(axis + d)], YR.at[ph, p, d - 1], axis_dev(d)) for d in (2, 1, 3)],
            ))
        yield
        x_groups = []
        for p in range(2):
            axis = rings[p][3]
            arrived(axis_groups[p])
            for a in range(2):
                v = ACC[p, axis, a]
                for i in range(3):
                    v = v + YR[ph, p, i, a].astype(F32)
                A2[ph, p, a] = v.astype(BF16)
            slot = XR.at[ph, p, myx]
            x_groups.append(send_all(XR.at[ph, p, 0:3], [
                (A2.at[ph, p, 1 - xh], slot, x_far),
                (A2.at[ph, p, 1 - xh], slot, x_pair),
                (A2.at[ph, p, xh], slot, x_same),
            ]))
            XR[ph, p, myx] = A2[ph, p, xh]
        yield
        for p in range(2):
            arrived(x_groups[p])
            terms = [XR[ph, p, i].astype(F32) for i in range(4)]
            out[p] = (terms[0] + terms[1]) + (terms[2] + terms[3])
            yield

    collected = {}
    flow = reduce_scatter(0, collected)
    next(flow)
    next(flow)
    next(flow)
    back = []
    for p in range(2):
        next(flow)
        part = slice(p * 32, p * 32 + 32)
        preact = own_scale[part] * collected[p]
        sig = 1.0 / (1.0 + jnp.exp(-preact))
        AS[part, :] = (preact * sig).astype(BF16)
        upstream = cot[pl.ds(pl.multiple_of(half + p * 32, 32), 32), :].astype(F32)
        grad = upstream * sig * (1.0 + preact * (1.0 - sig))
        XF[1, p, xh, z, y] = (own_scale[part] * grad).astype(BF16)
        back.append(all_gather(1, p))
        step([back[p]])
    act_group = send_all(AR, [(AS, AR, sib)])
    step(back)
    step(back)
    act_o[pl.ds(half, 64), :] = AS[...]
    arrived(act_group)
    act_o[pl.ds(other_half, 64), :] = AR[...]
    exchange = gather_sections(1, back)
    arrived(exchange[0])
    for k in (0, 1):
        early = G[1, k, 0:256] + GR[1, 1 - k, 0:256]
        arrived(exchange[1 + k])
        g = early + (LF[k] + LR[1 - k].astype(F32))
        if k == 0:
            gw_o[...] = jnp.sum(GATH[...] * g, axis=0, keepdims=True) * INV[0]
        MT[1, k] = ((SW[k] * INV[k]) * g).astype(BF16)

    mine = pl.ds(pl.multiple_of(core * 128, 128), 128)
    theirs = pl.ds(pl.multiple_of((1 - core) * 128, 128), 128)
    v = jnp.zeros((128, 256), F32)
    for k in range(2):
        v = v + dot(GH[k, mine, :], MT[1, k], NT) + dot(GL[k, mine, :], MT[1, k], NT)
    T0[...] = v.reshape(4, 4, 8, 256)
    theta_group = send_all(
        TP,
        [(T0.at[mod4(z + a), mod4(y + b)], TP.at[i], plane_dev[i]) for i, (a, b) in enumerate(plane)],
    )
    collected = {}
    flow = reduce_scatter(1, collected)
    next(flow)
    arrived(theta_group)
    v = T0[z, y]
    for i in range(15):
        v = v + TP[i]
    TX[myx] = v
    theta_group = send_all(TX.at[0:3], [(TX.at[myx], TX.at[myx], d) for d in (x_far, x_pair, x_same)])
    next(flow)
    arrived(theta_group)
    T3[z, y] = (TX[0] + TX[1]) + (TX[2] + TX[3])
    theta_group = send_all(TP, [(T3.at[z, y], T3.at[z, y], d) for d in plane_dev])
    next(flow)
    arrived(theta_group)
    theta_group = send_all(TS, [(T3, TS, sib)])
    gt_o[mine, :] = T3[...].reshape(128, 256)
    arrived(theta_group)
    gt_o[theirs, :] = TS[...].reshape(128, 256)
    for p in range(2):
        next(flow)
        part = slice(p * 32, p * 32 + 32)
        hi, lo = split(own_scale[part] * collected[p])
        FS[part, :] = (dot(hi, theta[...], NT) + dot(lo, theta[...], NT)).astype(BF16)
    grad_group = send_all(FR, [(FS, FR, sib)])
    gf_o[pl.ds(half, 64), :] = FS[...]
    arrived(grad_group)
    gf_o[pl.ds(other_half, 64), :] = FR[...]
    assert len(groups) == N_SEM, len(groups)
    for g in range(len(groups)):
        whole(g).wait_send()


def write_out(a, b, c, d, a_o, b_o, c_o, d_o, sem):
    pairs = [(a, a_o), (b, b_o), (c, c_o), (d, d_o)]
    copies = [pltpu.make_async_copy(src, dst, sem.at[i]) for i, (src, dst) in enumerate(pairs)]
    for copy in copies:
        copy.start()
    for copy in copies:
        copy.wait()


def body(features, theta, section_weight, pair_rows, pair_cols, pair_counts, cotangent):
    vmem = pl.BlockSpec(memory_space=pltpu.VMEM)
    hbm = pl.BlockSpec(memory_space=pltpu.HBM)

    def buf(shape, dtype):
        return pltpu.VMEM(shape, dtype)

    ins = (features, theta, section_weight.reshape(1, -1), pair_rows, pair_cols, pair_counts, cotangent)
    ins = [pltpu.with_memory_space_constraint(v, pltpu.HBM) for v in ins]
    outs = pl.pallas_call(
        layer,
        out_shape=(
            jax.ShapeDtypeStruct((128, 256), BF16),
            jax.ShapeDtypeStruct((128, 256), BF16),
            jax.ShapeDtypeStruct((256, 256), F32),
            jax.ShapeDtypeStruct((1, 512), F32),
        ),
        in_specs=[hbm] * 7,
        out_specs=(vmem, vmem, vmem, vmem),
        scratch_shapes=[
            buf((128, 256), BF16),
            buf((256, 256), BF16),
            buf((32, 512), jnp.int32),
            buf((32, 512), jnp.int32),
            pltpu.SMEM((1, 32), jnp.int32),
            buf((128, 256), BF16),
            buf((2, 2, 2, 4, 4, 32, 512), BF16),
            buf((2, 2, 4, 4, 32, 512), BF16),
            buf((8, 512), F32),
            buf((8, 512), F32),
            buf((16, 128), F32),
            buf((3, 16, 128), F32),
            buf((16, 128), F32),
            buf((15, 16, 128), F32),
            buf((128, 128), F32),
            buf((128, 128), F32),
            buf((2, 1, 512), F32),
            buf((2, 1, 512), F32),
            buf((2, 2, 2, 4, 4, 32, 256), BF16),
            buf((2, 2, 4, 4, 32, 128), F32),
            buf((2, 2, 272, 512), F32),
            buf((2, 2, 272, 512), F32),
            buf((2, 256, 512), F32),
            buf((2, 256, 512), BF16),
            buf((2, 256, 512), BF16),
            buf((2, 256, 512), BF16),
            buf((2, 256, 512), BF16),
            buf((256, 512), F32),
            buf((2, 2, 256, 512), BF16),
            buf((2, 2, 4, 32, 256), F32),
            buf((2, 2, 3, 2, 4, 32, 256), BF16),
            buf((2, 2, 3, 2, 4, 32, 256), BF16),
            buf((2, 4, 2, 32, 256), F32),
            buf((2, 2, 4, 2, 32, 256), BF16),
            buf((2, 2, 3, 2, 32, 256), BF16),
            buf((2, 2, 2, 32, 256), BF16),
            buf((2, 2, 4, 32, 256), BF16),
            buf((64, 256), BF16),
            buf((64, 256), BF16),
            buf((64, 256), BF16),
            buf((64, 256), BF16),
            buf((256, 256), BF16),
            buf((4, 4, 8, 256), F32),
            buf((15, 8, 256), F32),
            buf((4, 8, 256), F32),
            buf((4, 4, 8, 256), F32),
            buf((4, 4, 8, 256), F32),
            pltpu.SemaphoreType.DMA((N_SEM,)),
            pltpu.SemaphoreType.DMA((N_SEM,)),
            pltpu.SemaphoreType.DMA((7,)),
        ],
        compiler_params=pltpu.CompilerParams(
            collective_id=0, has_side_effects=True, vmem_limit_bytes=40 * 1024 * 1024
        ),
    )(*ins)
    anywhere = pl.BlockSpec(memory_space=pl.ANY)
    outs = pl.pallas_call(
        write_out,
        out_shape=tuple(jax.ShapeDtypeStruct(o.shape, o.dtype) for o in outs),
        in_specs=[vmem] * 4,
        out_specs=(anywhere,) * 4,
        scratch_shapes=[pltpu.SemaphoreType.DMA((4,))],
        compiler_params=pltpu.CompilerParams(vmem_limit_bytes=4 * 1024 * 1024),
    )(*outs)
    return outs[0], outs[1], outs[2], outs[3].reshape(-1)


def solution(mesh):
    placed = (
        P("ent", None),
        P(),
        P(("ent", "sec")),
        P(("ent", "sec"), None, None),
        P(("ent", "sec"), None, None),
        P(("ent", "sec"), None),
        P("ent", None),
    )
    return jax.shard_map(
        body,
        mesh=mesh,
        in_specs=placed,
        out_specs=(P("ent", None), P("ent", None), P(), P(("ent", "sec"))),
        check_vma=False,
    )
```

```python
import functools

import jax
import jax.numpy as jnp
from jax import lax
from jax.experimental import pallas as pl
from jax.experimental.pallas import tpu as pltpu
from jax.sharding import PartitionSpec as P

F32 = jnp.float32
BF16 = jnp.bfloat16
F8 = jnp.float8_e4m3fn
MESH = pl.DeviceIdType.MESH
NT = (((1,), (1,)), ((), ()))
NN = (((1,), (0,)), ((), ()))
N_SEM = 73


def dot(a, b, dims):
    return lax.dot_general(a, b, dims, preferred_element_type=F32)


def split(v):
    hi = v.astype(BF16)
    return hi, (v - hi.astype(F32)).astype(BF16)


def layer(
    feat_h, theta_h, sw_h, rows_h, cols_h, counts_h, cot_h,
    act_o, gf_o, gt_o, gw_o,
    feat, theta, rows, cols, counts, cot,
    HT, HS, DS, DR, D1, DX, D2, DP, DW, DT, SW, INV, XF, XB, SC, G, GR, LF, LB, LR, GH, GL, GATH, MT, PF, PB,
    RB, ACC, YS, YR, A2, XR, AS, AR, FS, FR, TH,
    T0, TP, TX, T3, TS, ssem, rsem, lsem,
):
    e = lax.axis_index("ent")
    s = lax.axis_index("sec")
    core = lax.rem(s, 2)
    xl = lax.div(s, 2)
    xh = lax.div(e, 16)
    z = lax.rem(lax.div(e, 4), 4)
    y = lax.rem(e, 4)
    myx = xh * 2 + xl
    half = pl.multiple_of(core * 64, 64)
    other_half = pl.multiple_of((1 - core) * 64, 64)

    loads = [
        pltpu.make_async_copy(src, dst, lsem.at[i])
        for i, (src, dst) in enumerate([
            (feat_h, feat), (cols_h.at[0], cols), (counts_h, counts), (rows_h.at[0], rows),
            (sw_h, SW.at[0]), (theta_h, theta), (cot_h, cot),
        ])
    ]
    for copy in loads:
        copy.start()

    def dev(xh_, xl_, z_, y_):
        return (xh_ * 16 + z_ * 4 + y_, xl_ * 2 + core)

    def mod4(v):
        return lax.rem(v + 4, 4)

    sib = (e, xl * 2 + 1 - core)
    x_pair = dev(1 - xh, 1 - xl, z, y)
    x_far = dev(1 - xh, xl, z, y)
    x_same = dev(xh, 1 - xl, z, y)

    def z_dev(d):
        return dev(xh, xl, mod4(z + d), y)

    def y_dev(d):
        return dev(xh, xl, z, mod4(y + d))

    plane = [(a, b) for a in range(4) for b in range(4) if a or b]
    plane.sort(key=lambda ab: -(min(ab[0], 4 - ab[0]) + min(ab[1], 4 - ab[1])))
    plane_dev = [dev(xh, xl, mod4(z + a), mod4(y + b)) for a, b in plane]
    pair_z = [dev(1 - xh, 1 - xl, mod4(z + d), y) for d in range(4)]
    pair_y = [dev(1 - xh, 1 - xl, z, mod4(y + d)) for d in range(4)]
    peers = [sib, x_pair, x_far, x_same] + plane_dev + pair_z[1:] + pair_y[1:]
    groups = []

    def open_group(size):
        groups.append(size)
        return len(groups) - 1

    def send(g, src, dst, device):
        pltpu.make_async_remote_copy(
            src_ref=src, dst_ref=dst, send_sem=ssem.at[g], recv_sem=rsem.at[g],
            device_id=device, device_id_type=MESH,
        ).start()

    def whole(g):
        return pltpu.make_async_remote_copy(
            src_ref=groups[g], dst_ref=groups[g], send_sem=ssem.at[g], recv_sem=rsem.at[g],
            device_id=sib, device_id_type=MESH,
        )

    def send_all(size, copies):
        g = open_group(size)
        for src, dst, device in copies:
            send(g, src, dst, device)
        return g

    def arrived(g):
        whole(g).wait_recv()

    barrier = pltpu.get_barrier_semaphore()
    for peer in peers:
        pl.semaphore_signal(barrier, inc=1, device_id=peer, device_id_type=MESH)

    slot_row = lax.broadcasted_iota(jnp.int32, (1, 512), 1)
    ent_iota = lax.broadcasted_iota(jnp.int32, (128, 512), 0)

    def col_table(j):
        live = slot_row < counts[0, j]
        col = jnp.where(live, cols[pl.ds(j, 1), :], -1)
        return jnp.where(ent_iota == col, 1.0, 0.0).astype(F8)

    for copy in loads[1:3]:
        copy.wait()
    ones = jnp.ones((8, 512), F8)
    for k in range(8):
        table = jnp.concatenate([col_table(4 * k + i) for i in range(4)], axis=0)
        DS[k:k + 1, :] = dot(ones, table, NT)[0:1]

    loads[0].wait()
    for p in range(2):
        XF[p, xh, z, y] = feat[pl.ds(pl.multiple_of(half + 32 * p, 32), 32), :]

    pl.semaphore_wait(barrier, len(peers))

    def all_gather(buf, p):
        near_dev, pair_dev, ring_dev = (y_dev, pair_y, z_dev) if p == 0 else (z_dev, pair_z, y_dev)

        def line(a):
            return buf.at[a, z] if p == 0 else buf.at[a, :, y]

        own = buf.at[xh, z, y]
        same = send_all(buf.at[0, 0, 0:3], [(own, own, near_dev(d)) for d in (2, 1, 3)])
        pair = send_all(buf.at[0, 0], [(own, own, pair_dev[d]) for d in (2, 1, 3, 0)])
        rings = {d: open_group(buf.at[0, 0:2]) for d in (1, 3, 2)}
        yield
        for stage, a in ((same, xh), (pair, 1 - xh)):
            arrived(stage)
            for d in (1, 3, 2):
                send(rings[d], line(a), line(a), ring_dev(d))
            yield
        for d in (1, 3, 2):
            arrived(rings[d])
            yield

    def degree_sum():
        m = send_all(DR, [(DS, DR, sib)])
        yield
        arrived(m)
        v = DS[...] + DR[...]
        v = jnp.concatenate([v[:, i * 128:(i + 1) * 128] for i in range(4)], axis=0)
        v = jnp.where(core == 0, v[:, 0:64], v[:, 64:128])
        D1[...] = jnp.concatenate([v[0:16], v[16:32]], axis=1)
        m = send_all(DX, [(D1, DX.at[i], d) for i, d in enumerate((x_pair, x_same, x_far))])
        yield
        arrived(m)
        D2[...] = D1[...] + DX[0] + DX[1] + DX[2]
        m = send_all(DP, [(D2, DP.at[i], d) for i, d in enumerate(plane_dev)])
        yield
        arrived(m)
        v = D2[...]
        for i in range(15):
            v = v + DP[i]
        DW[...] = jnp.zeros((128, 128), F32)
        DW[0:16, :] = lax.rsqrt(1.0 + v)
        DT[...] = DW[...].T
        yield

    def step(gens):
        for g in gens:
            next(g, None)

    degrees = degree_sum()
    step([degrees])
    gathers = [all_gather(XF.at[p], p) for p in range(2)]
    step(gathers)
    loads[3].wait()

    sec_iota = lax.broadcasted_iota(jnp.int32, (512, 512), 0)

    table_group = open_group(HS)

    def table_line(k):
        a, b = k // 4, k % 4

        def table_block(i, carry):
            j = 4 * k + i
            row_hot = jnp.where(sec_iota == rows[pl.ds(j, 1), :], 1.0, 0.0).astype(F8)
            block = dot(col_table(j), row_hot, NT).astype(BF16)
            for h in range(2):
                for p in range(2):
                    HT[h, p, a, b, i] = block[h * 64 + p * 32:h * 64 + p * 32 + 32]
            return carry

        lax.fori_loop(0, 4, table_block, 0)
        send(table_group, HT.at[1 - core, :, a, b], HS.at[:, a, b], sib)

    step([degrees])
    for k in range(3):
        table_line(k)
    step([degrees])
    step(gathers)
    step(gathers)
    loads[4].wait()
    sw_group = send_all(SW.at[1], [(SW.at[0], SW.at[1], sib)])
    for k in range(3, 8):
        table_line(k)
    for copy in loads[5:]:
        copy.wait()
    TH[...] = theta[...].T
    step([degrees])
    cols_of = [DT[0:64, 0:16], DT[64:128, 0:16]]
    for c in range(4):
        for a in range(2):
            for b in range(4):
                r = c * 8 + a * 4 + b
                column = cols_of[r // 16][:, r % 16:r % 16 + 1]
                for p in range(2):
                    SC[p, a, b, c] = jnp.broadcast_to(column[p * 32:p * 32 + 32], (32, 128))

    own_scale = jnp.concatenate([SC[p, xh, z, y] for p in range(2)], axis=0)

    def table_rows(p, i, k):
        ref = HT.at[core, p] if k == 0 else HS.at[p]
        pieces = [(ref[a, i] if p == 0 else ref[a, :, i]).reshape(128, 512) for a in range(2)]
        return jnp.concatenate(pieces, axis=0)

    def core_sum(src, dst):
        return send_all(dst, [(src, dst, sib)])

    def line_of(ref, p, a, i):
        return ref[p, a, i] if p == 0 else ref[p, a, :, i]

    def scaled_line(p, i):
        pieces = []
        for a in range(2):
            v = line_of(XF, p, a, i).reshape(128, 256)
            scale = line_of(SC, p, a, i).reshape(128, 128)
            pieces.append((v.astype(F32) * jnp.concatenate([scale, scale], axis=1)).astype(BF16))
        xt = jnp.concatenate(pieces, axis=0).T
        return jnp.concatenate([xt, jnp.ones((16, 256), BF16)], axis=0)

    def back_line(q, p, i):
        pieces = [line_of(XB.at[q], p, a, i).reshape(128, 128) for a in range(2)]
        return jnp.concatenate(pieces, axis=0).T

    def lines_dot(line, d, k):
        total = None
        for p, i in enumerate((mod4(z + d), mod4(y + d))):
            t = dot(line(p, i), table_rows(p, i, k), NN)
            total = t if total is None else total + t
        return total

    arrived(table_group)
    arrived(sw_group)
    for k in range(2):
        G[0, k] = lines_dot(scaled_line, 0, k)
    for d in (3, 1):
        step(gathers)
        for k in range(2):
            G[0, k] += lines_dot(scaled_line, d, k)
    step(gathers)
    exchange = []
    for k in (1, 0):
        G[0, k] += lines_dot(scaled_line, 2, k)
        exchange.append(core_sum(G.at[0, k], GR.at[0, k]))
    for k in (0, 1):
        arrived(exchange[k])
        g = G[0, k] + GR[0, 1 - k]
        inverse = 1.0 / (1.0 + g[256:257])
        INV[k] = inverse
        hi, lo = split(g[0:256])
        GH[k] = hi
        GL[k] = lo
        gathered = dot(TH[...], hi, NN) + dot(TH[...], lo, NN)
        if k == 0:
            GATH[...] = gathered
        MT[0, k] = ((SW[k] * inverse) * gathered).astype(BF16)

    lanes = [slice(q * 128, q * 128 + 128) for q in range(2)]

    def reduce_scatter(ph, q, out):
        rings = [(z_dev, y_dev, z, y), (y_dev, z_dev, y, z)]
        pb, rb, ys, yr, a2, xr = [ref.at[ph, q] for ref in (PB, RB, YS, YR, A2, XR)]
        pf, acc = PF.at[q], ACC.at[q]
        rhs = [MT[ph, k, lanes[q], :] for k in range(2)]

        def term(p, i):
            return dot(table_rows(p, i, 0), rhs[0], NT) + dot(table_rows(p, i, 1), rhs[1], NT)

        ring_groups = [open_group(rb.at[p]) for p in range(2)]
        for m, d in enumerate((2, 1, 3)):
            for p in range(2):
                ring_dev, _, ring, _ = rings[p]
                pb[p, m] = term(p, mod4(ring + d)).astype(BF16).reshape(2, 4, 32, 128)
                send(ring_groups[p], pb.at[p, m], rb.at[p, m], ring_dev(d))
        for p in range(2):
            pf[p] = term(p, rings[p][2]).reshape(2, 4, 32, 128)
        yield
        axis_groups = []
        for p in range(2):
            _, axis_dev, _, axis = rings[p]
            arrived(ring_groups[p])
            for o in range(4):
                for a in range(2):
                    v = pf[p, a, o]
                    for m in range(3):
                        v = v + rb[p, m, a, o].astype(F32)
                    acc[p, o, a] = v
                    ys[p, o, a] = v.astype(BF16)
            axis_groups.append(send_all(
                yr.at[p],
                [(ys.at[p, mod4(axis + d)], yr.at[p, d - 1], axis_dev(d)) for d in (2, 1, 3)],
            ))
        yield
        x_groups = []
        for p in range(2):
            axis = rings[p][3]
            arrived(axis_groups[p])
            for a in range(2):
                v = acc[p, axis, a]
                for i in range(3):
                    v = v + yr[p, i, a].astype(F32)
                a2[p, a] = v.astype(BF16)
            slot = xr.at[p, myx]
            x_groups.append(send_all(xr.at[p, 0:3], [
                (a2.at[p, 1 - xh], slot, x_far),
                (a2.at[p, 1 - xh], slot, x_pair),
                (a2.at[p, xh], slot, x_same),
            ]))
            xr[p, myx] = a2[p, xh]
        yield
        for p in range(2):
            arrived(x_groups[p])
            terms = [xr[p, i].astype(F32) for i in range(4)]
            out[p] = (terms[0] + terms[1]) + (terms[2] + terms[3])
            yield

    collected = [{}, {}]
    flows = [reduce_scatter(0, q, collected[q]) for q in range(2)]
    for _ in range(3):
        step(flows)
    back = []
    for q in range(2):
        back.append([])
        for p in range(2):
            next(flows[q])
            part = slice(p * 32, p * 32 + 32)
            preact = own_scale[part] * collected[q][p]
            sig = 1.0 / (1.0 + jnp.exp(-preact))
            AS[part, lanes[q]] = (preact * sig).astype(BF16)
            upstream = cot[pl.ds(pl.multiple_of(half + p * 32, 32), 32), lanes[q]].astype(F32)
            grad = upstream * sig * (1.0 + preact * (1.0 - sig))
            XB[q, p, xh, z, y] = (own_scale[part] * grad).astype(BF16)
            back[q].append(all_gather(XB.at[q, p], p))
            step([back[q][p]])
    act_group = send_all(AR, [(AS, AR, sib)])
    for _ in range(2):
        for q in range(2):
            step(back[q])
    act_o[pl.ds(half, 64), :] = AS[...]
    arrived(act_group)
    act_o[pl.ds(other_half, 64), :] = AR[...]

    exchange = [[], []]
    line_q = [functools.partial(back_line, q) for q in range(2)]

    def early_lines(q, d):
        if d:
            step(back[q])
        for k in range(2):
            v = lines_dot(line_q[q], d, k)
            if d:
                v = v + G[1, k, lanes[q]]
            G[1, k, lanes[q]] = v

    def early_exchange(q):
        exchange[q].append(core_sum(G.at[1, :, lanes[q]], GR.at[1, :, lanes[q]]))

    def last_lines(q):
        step(back[q])
        for k in (1, 0):
            v = lines_dot(line_q[q], 2, k)
            LF[k, lanes[q]] = v
            LB[q, k] = v.astype(BF16)
            exchange[q].append(core_sum(LB.at[q, k], LR.at[q, k]))

    weight_terms = []

    def back_messages(q):
        arrived(exchange[q][0])
        for k in range(2):
            early = G[1, k, lanes[q]] + GR[1, 1 - k, lanes[q]]
            arrived(exchange[q][1 + k])
            g = early + (LF[k, lanes[q]] + LR[q, 1 - k].astype(F32))
            if k == 0:
                weight_terms.append(jnp.sum(GATH[lanes[q]] * g, axis=0, keepdims=True))
            MT[1, k, lanes[q], :] = ((SW[k] * INV[k]) * g).astype(BF16)

    for d in (0, 3):
        for q in range(2):
            early_lines(q, d)
    for q in range(2):
        early_lines(q, 1)
        early_exchange(q)
    collected = [{}, {}]
    flows = [reduce_scatter(1, q, collected[q]) for q in range(2)]
    last_lines(0)
    back_messages(0)
    last_lines(1)
    next(flows[0])
    back_messages(1)
    mine = pl.ds(pl.multiple_of(core * 128, 128), 128)
    theirs = pl.ds(pl.multiple_of((1 - core) * 128, 128), 128)
    v = jnp.zeros((128, 256), F32)
    for k in range(2):
        v = v + dot(GH[k, mine, :], MT[1, k], NT) + dot(GL[k, mine, :], MT[1, k], NT)
    T0[...] = v.reshape(4, 4, 8, 256)
    theta_group = send_all(
        TP,
        [(T0.at[mod4(z + a), mod4(y + b)], TP.at[i], plane_dev[i]) for i, (a, b) in enumerate(plane)],
    )
    next(flows[1])
    gw_o[...] = (weight_terms[0] + weight_terms[1]) * INV[0]

    next(flows[0])
    arrived(theta_group)
    v = T0[z, y]
    for i in range(15):
        v = v + TP[i]
    TX[myx] = v
    theta_group = send_all(TX.at[0:3], [(TX.at[myx], TX.at[myx], d) for d in (x_far, x_pair, x_same)])
    next(flows[1])
    next(flows[0])
    arrived(theta_group)
    T3[z, y] = (TX[0] + TX[1]) + (TX[2] + TX[3])
    theta_group = send_all(TP, [(T3.at[z, y], T3.at[z, y], d) for d in plane_dev])
    next(flows[1])
    done = len(groups) - 5
    for g in range(done):
        whole(g).wait_send()
    arrived(theta_group)
    theta_group = send_all(TS, [(T3, TS, sib)])
    gt_o[mine, :] = T3[...].reshape(128, 256)
    arrived(theta_group)
    gt_o[theirs, :] = TS[...].reshape(128, 256)
    for p in range(2):
        step(flows)
        part = slice(p * 32, p * 32 + 32)
        proj = jnp.concatenate([own_scale[part] * collected[q][p] for q in range(2)], axis=1)
        hi, lo = split(proj)
        FS[part, :] = (dot(hi, theta[...], NT) + dot(lo, theta[...], NT)).astype(BF16)
    grad_group = send_all(FR, [(FS, FR, sib)])
    gf_o[pl.ds(half, 64), :] = FS[...]
    arrived(grad_group)
    gf_o[pl.ds(other_half, 64), :] = FR[...]
    assert len(groups) == N_SEM, len(groups)
    for g in range(done, len(groups)):
        whole(g).wait_send()


def write_out(a, b, c, d, a_o, b_o, c_o, d_o, sem):
    pairs = [(a, a_o), (b, b_o), (c, c_o), (d, d_o)]
    copies = [pltpu.make_async_copy(src, dst, sem.at[i]) for i, (src, dst) in enumerate(pairs)]
    for copy in copies:
        copy.start()
    for copy in copies:
        copy.wait()


def body(features, theta, section_weight, pair_rows, pair_cols, pair_counts, cotangent):
    vmem = pl.BlockSpec(memory_space=pltpu.VMEM)
    hbm = pl.BlockSpec(memory_space=pltpu.HBM)

    def buf(shape, dtype):
        return pltpu.VMEM(shape, dtype)

    ins = (features, theta, section_weight.reshape(1, -1), pair_rows, pair_cols, pair_counts, cotangent)
    ins = [pltpu.with_memory_space_constraint(v, pltpu.HBM) for v in ins]
    outs = pl.pallas_call(
        layer,
        out_shape=(
            jax.ShapeDtypeStruct((128, 256), BF16),
            jax.ShapeDtypeStruct((128, 256), BF16),
            jax.ShapeDtypeStruct((256, 256), F32),
            jax.ShapeDtypeStruct((1, 512), F32),
        ),
        in_specs=[hbm] * 7,
        out_specs=(vmem, vmem, vmem, vmem),
        scratch_shapes=[
            buf((128, 256), BF16),
            buf((256, 256), BF16),
            buf((32, 512), jnp.int32),
            buf((32, 512), jnp.int32),
            pltpu.SMEM((1, 32), jnp.int32),
            buf((128, 256), BF16),
            buf((2, 2, 2, 4, 4, 32, 512), BF16),
            buf((2, 2, 4, 4, 32, 512), BF16),
            buf((8, 512), F32),
            buf((8, 512), F32),
            buf((16, 128), F32),
            buf((3, 16, 128), F32),
            buf((16, 128), F32),
            buf((15, 16, 128), F32),
            buf((128, 128), F32),
            buf((128, 128), F32),
            buf((2, 1, 512), F32),
            buf((2, 1, 512), F32),
            buf((2, 2, 4, 4, 32, 256), BF16),
            buf((2, 2, 2, 4, 4, 32, 128), BF16),
            buf((2, 2, 4, 4, 32, 128), F32),
            buf((2, 2, 272, 512), F32),
            buf((2, 2, 272, 512), F32),
            buf((2, 256, 512), F32),
            buf((2, 2, 128, 512), BF16),
            buf((2, 2, 128, 512), BF16),
            buf((2, 256, 512), BF16),
            buf((2, 256, 512), BF16),
            buf((256, 512), F32),
            buf((2, 2, 256, 512), BF16),
            buf((2, 2, 2, 4, 32, 128), F32),
            buf((2, 2, 2, 3, 2, 4, 32, 128), BF16),
            buf((2, 2, 2, 3, 2, 4, 32, 128), BF16),
            buf((2, 2, 4, 2, 32, 128), F32),
            buf((2, 2, 2, 4, 2, 32, 128), BF16),
            buf((2, 2, 2, 3, 2, 32, 128), BF16),
            buf((2, 2, 2, 2, 32, 128), BF16),
            buf((2, 2, 2, 4, 32, 128), BF16),
            buf((64, 256), BF16),
            buf((64, 256), BF16),
            buf((64, 256), BF16),
            buf((64, 256), BF16),
            buf((256, 256), BF16),
            buf((4, 4, 8, 256), F32),
            buf((15, 8, 256), F32),
            buf((4, 8, 256), F32),
            buf((4, 4, 8, 256), F32),
            buf((4, 4, 8, 256), F32),
            pltpu.SemaphoreType.DMA((N_SEM,)),
            pltpu.SemaphoreType.DMA((N_SEM,)),
            pltpu.SemaphoreType.DMA((7,)),
        ],
        compiler_params=pltpu.CompilerParams(
            collective_id=0, has_side_effects=True, vmem_limit_bytes=40 * 1024 * 1024
        ),
    )(*ins)
    anywhere = pl.BlockSpec(memory_space=pl.ANY)
    outs = pl.pallas_call(
        write_out,
        out_shape=tuple(jax.ShapeDtypeStruct(o.shape, o.dtype) for o in outs),
        in_specs=[vmem] * 4,
        out_specs=(anywhere,) * 4,
        scratch_shapes=[pltpu.SemaphoreType.DMA((4,))],
        compiler_params=pltpu.CompilerParams(vmem_limit_bytes=4 * 1024 * 1024),
    )(*outs)
    return outs[0], outs[1], outs[2], outs[3].reshape(-1)


def solution(mesh):
    placed = (
        P("ent", None),
        P(),
        P(("ent", "sec")),
        P(("ent", "sec"), None, None),
        P(("ent", "sec"), None, None),
        P(("ent", "sec"), None),
        P("ent", None),
    )
    return jax.shard_map(
        body,
        mesh=mesh,
        in_specs=placed,
        out_specs=(P("ent", None), P("ent", None), P(), P(("ent", "sec"))),
        check_vma=False,
    )
```

```python
import functools

import jax
import jax.numpy as jnp
from jax import lax
from jax.experimental import pallas as pl
from jax.experimental.pallas import tpu as pltpu
from jax.sharding import PartitionSpec as P

F32 = jnp.float32
BF16 = jnp.bfloat16
F8 = jnp.float8_e4m3fn
MESH = pl.DeviceIdType.MESH
NT = (((1,), (1,)), ((), ()))
NN = (((1,), (0,)), ((), ()))
N_SEM = 73


def dot(a, b, dims):
    return lax.dot_general(a, b, dims, preferred_element_type=F32)


def split(v):
    hi = v.astype(BF16)
    return hi, (v - hi.astype(F32)).astype(BF16)


def layer(
    feat_h, theta_h, sw_h, rows_h, cols_h, counts_h, cot_h,
    act_o, gf_o, gt_o, gw_o,
    feat, theta, rows, cols, counts, cot,
    HT, HS, DS, DR, D1, DX, D2, DP, DW, DT, SW, INV, XF, XB, SC, G, GR, LF, LB, LR, GH, GL, GATH, MT, PF, PB,
    RB, ACC, YS, YR, A2, XR, AS, AR, FS, FR, TH,
    T0, TP, TX, T3, TS, ssem, rsem, lsem,
):
    e = lax.axis_index("ent")
    s = lax.axis_index("sec")
    core = lax.rem(s, 2)
    xl = lax.div(s, 2)
    xh = lax.div(e, 16)
    z = lax.rem(lax.div(e, 4), 4)
    y = lax.rem(e, 4)
    myx = xh * 2 + xl
    half = pl.multiple_of(core * 64, 64)
    other_half = pl.multiple_of((1 - core) * 64, 64)

    loads = [
        pltpu.make_async_copy(src, dst, lsem.at[i])
        for i, (src, dst) in enumerate([
            (feat_h, feat), (cols_h.at[0], cols), (counts_h, counts), (rows_h.at[0], rows),
            (sw_h, SW.at[0]), (theta_h, theta), (cot_h, cot),
        ])
    ]
    for copy in loads:
        copy.start()

    def dev(xh_, xl_, z_, y_):
        return (xh_ * 16 + z_ * 4 + y_, xl_ * 2 + core)

    def mod4(v):
        return lax.rem(v + 4, 4)

    sib = (e, xl * 2 + 1 - core)
    x_pair = dev(1 - xh, 1 - xl, z, y)
    x_far = dev(1 - xh, xl, z, y)
    x_same = dev(xh, 1 - xl, z, y)

    def z_dev(d):
        return dev(xh, xl, mod4(z + d), y)

    def y_dev(d):
        return dev(xh, xl, z, mod4(y + d))

    plane = [(a, b) for a in range(4) for b in range(4) if a or b]
    plane.sort(key=lambda ab: -(min(ab[0], 4 - ab[0]) + min(ab[1], 4 - ab[1])))
    plane_dev = [dev(xh, xl, mod4(z + a), mod4(y + b)) for a, b in plane]
    pair_z = [dev(1 - xh, 1 - xl, mod4(z + d), y) for d in range(4)]
    pair_y = [dev(1 - xh, 1 - xl, z, mod4(y + d)) for d in range(4)]
    peers = [sib, x_pair, x_far, x_same] + plane_dev + pair_z[1:] + pair_y[1:]
    groups = []

    def open_group(size):
        groups.append(size)
        return len(groups) - 1

    def send(g, src, dst, device):
        pltpu.make_async_remote_copy(
            src_ref=src, dst_ref=dst, send_sem=ssem.at[g], recv_sem=rsem.at[g],
            device_id=device, device_id_type=MESH,
        ).start()

    def whole(g):
        return pltpu.make_async_remote_copy(
            src_ref=groups[g], dst_ref=groups[g], send_sem=ssem.at[g], recv_sem=rsem.at[g],
            device_id=sib, device_id_type=MESH,
        )

    def send_all(size, copies):
        g = open_group(size)
        for src, dst, device in copies:
            send(g, src, dst, device)
        return g

    def arrived(g):
        whole(g).wait_recv()

    barrier = pltpu.get_barrier_semaphore()
    for peer in peers:
        pl.semaphore_signal(barrier, inc=1, device_id=peer, device_id_type=MESH)

    slot_row = lax.broadcasted_iota(jnp.int32, (1, 512), 1)
    ent_iota = lax.broadcasted_iota(jnp.int32, (128, 512), 0)

    def col_table(j):
        live = slot_row < counts[0, j]
        col = jnp.where(live, cols[pl.ds(j, 1), :], -1)
        return jnp.where(ent_iota == col, 1.0, 0.0).astype(F8)

    for copy in loads[1:3]:
        copy.wait()
    ones = jnp.ones((8, 512), F8)
    for k in range(8):
        table = jnp.concatenate([col_table(4 * k + i) for i in range(4)], axis=0)
        DS[k:k + 1, :] = dot(ones, table, NT)[0:1]

    loads[0].wait()
    for p in range(2):
        XF[p, xh, z, y] = feat[pl.ds(pl.multiple_of(half + 32 * p, 32), 32), :]

    pl.semaphore_wait(barrier, len(peers))

    def all_gather(buf, p):
        near_dev, pair_dev, ring_dev = (y_dev, pair_y, z_dev) if p == 0 else (z_dev, pair_z, y_dev)

        def line(a):
            return buf.at[a, z] if p == 0 else buf.at[a, :, y]

        own = buf.at[xh, z, y]
        same = send_all(buf.at[0, 0, 0:3], [(own, own, near_dev(d)) for d in (2, 1, 3)])
        pair = send_all(buf.at[0, 0], [(own, own, pair_dev[d]) for d in (2, 1, 3, 0)])
        rings = {d: open_group(buf.at[0, 0:2]) for d in (2, 1, 3)}
        yield
        for stage, a in ((same, xh), (pair, 1 - xh)):
            arrived(stage)
            for d in (2, 1, 3):
                send(rings[d], line(a), line(a), ring_dev(d))
            yield
        for d in (2, 1, 3):
            arrived(rings[d])
            yield

    def degree_sum():
        m = send_all(DR, [(DS, DR, sib)])
        yield
        arrived(m)
        v = DS[...] + DR[...]
        v = jnp.concatenate([v[:, i * 128:(i + 1) * 128] for i in range(4)], axis=0)
        v = jnp.where(core == 0, v[:, 0:64], v[:, 64:128])
        D1[...] = jnp.concatenate([v[0:16], v[16:32]], axis=1)
        m = send_all(DX, [(D1, DX.at[i], d) for i, d in enumerate((x_pair, x_same, x_far))])
        yield
        arrived(m)
        D2[...] = D1[...] + DX[0] + DX[1] + DX[2]
        m = send_all(DP, [(D2, DP.at[i], d) for i, d in enumerate(plane_dev)])
        yield
        arrived(m)
        v = D2[...]
        for i in range(15):
            v = v + DP[i]
        DW[...] = jnp.zeros((128, 128), F32)
        DW[0:16, :] = lax.rsqrt(1.0 + v)
        DT[...] = DW[...].T
        yield

    def step(gens):
        for g in gens:
            next(g, None)

    degrees = degree_sum()
    step([degrees])
    gathers = [all_gather(XF.at[p], p) for p in range(2)]
    step(gathers)
    loads[3].wait()

    sec_iota = lax.broadcasted_iota(jnp.int32, (512, 512), 0)

    table_group = open_group(HS)

    def table_line(k):
        a, b = k // 4, k % 4

        def table_block(i, carry):
            j = 4 * k + i
            row_hot = jnp.where(sec_iota == rows[pl.ds(j, 1), :], 1.0, 0.0).astype(F8)
            block = dot(col_table(j), row_hot, NT).astype(BF16)
            for h in range(2):
                for p in range(2):
                    HT[h, p, a, b, i] = block[h * 64 + p * 32:h * 64 + p * 32 + 32]
            return carry

        lax.fori_loop(0, 4, table_block, 0)
        send(table_group, HT.at[1 - core, :, a, b], HS.at[:, a, b], sib)

    step([degrees])
    for k in range(2):
        table_line(k)
    step([degrees])
    step(gathers)
    step(gathers)
    loads[4].wait()
    sw_group = send_all(SW.at[1], [(SW.at[0], SW.at[1], sib)])
    for k in range(2, 8):
        table_line(k)
    for copy in loads[5:]:
        copy.wait()
    TH[...] = theta[...].T
    step([degrees])
    cols_of = [DT[0:64, 0:16], DT[64:128, 0:16]]
    for c in range(4):
        for a in range(2):
            for b in range(4):
                r = c * 8 + a * 4 + b
                column = cols_of[r // 16][:, r % 16:r % 16 + 1]
                for p in range(2):
                    SC[p, a, b, c] = jnp.broadcast_to(column[p * 32:p * 32 + 32], (32, 128))

    own_scale = jnp.concatenate([SC[p, xh, z, y] for p in range(2)], axis=0)

    def table_rows(p, i, k):
        ref = HT.at[core, p] if k == 0 else HS.at[p]
        pieces = [(ref[a, i] if p == 0 else ref[a, :, i]).reshape(128, 512) for a in range(2)]
        return jnp.concatenate(pieces, axis=0)

    def core_sum(src, dst):
        return send_all(dst, [(src, dst, sib)])

    def line_of(ref, p, a, i):
        return ref[p, a, i] if p == 0 else ref[p, a, :, i]

    def scaled_line(p, i):
        pieces = []
        for a in range(2):
            v = line_of(XF, p, a, i).reshape(128, 256)
            scale = line_of(SC, p, a, i).reshape(128, 128)
            pieces.append((v.astype(F32) * jnp.concatenate([scale, scale], axis=1)).astype(BF16))
        xt = jnp.concatenate(pieces, axis=0).T
        return jnp.concatenate([xt, jnp.ones((16, 256), BF16)], axis=0)

    def back_line(q, p, i):
        pieces = [line_of(XB.at[q], p, a, i).reshape(128, 128) for a in range(2)]
        return jnp.concatenate(pieces, axis=0).T

    def lines_dot(line, d, k):
        total = None
        for p, i in enumerate((mod4(z + d), mod4(y + d))):
            t = dot(line(p, i), table_rows(p, i, k), NN)
            total = t if total is None else total + t
        return total

    arrived(table_group)
    arrived(sw_group)
    for k in range(2):
        G[0, k] = lines_dot(scaled_line, 0, k)
    for d in (2, 3):
        step(gathers)
        for k in range(2):
            G[0, k] += lines_dot(scaled_line, d, k)
    step(gathers)
    exchange = []
    for k in (1, 0):
        G[0, k] += lines_dot(scaled_line, 1, k)
        exchange.append(core_sum(G.at[0, k], GR.at[0, k]))
    for k in (0, 1):
        arrived(exchange[k])
        g = G[0, k] + GR[0, 1 - k]
        inverse = 1.0 / (1.0 + g[256:257])
        INV[k] = inverse
        hi, lo = split(g[0:256])
        GH[k] = hi
        GL[k] = lo
        gathered = dot(TH[...], hi, NN) + dot(TH[...], lo, NN)
        if k == 0:
            GATH[...] = gathered
        MT[0, k] = ((SW[k] * inverse) * gathered).astype(BF16)

    lanes = [slice(q * 128, q * 128 + 128) for q in range(2)]

    def reduce_scatter(ph, q, out):
        rings = [(z_dev, y_dev, z, y), (y_dev, z_dev, y, z)]
        pb, rb, ys, yr, a2, xr = [ref.at[ph, q] for ref in (PB, RB, YS, YR, A2, XR)]
        pf, acc = PF.at[q], ACC.at[q]
        rhs = [MT[ph, k, lanes[q], :] for k in range(2)]

        def term(p, i):
            return dot(table_rows(p, i, 0), rhs[0], NT) + dot(table_rows(p, i, 1), rhs[1], NT)

        ring_groups = [open_group(rb.at[p]) for p in range(2)]
        for m, d in enumerate((2, 1, 3)):
            for p in range(2):
                ring_dev, _, ring, _ = rings[p]
                pb[p, m] = term(p, mod4(ring + d)).astype(BF16).reshape(2, 4, 32, 128)
                send(ring_groups[p], pb.at[p, m], rb.at[p, m], ring_dev(d))
        for p in range(2):
            pf[p] = term(p, rings[p][2]).reshape(2, 4, 32, 128)
        yield
        axis_groups = []
        for p in range(2):
            _, axis_dev, _, axis = rings[p]
            arrived(ring_groups[p])
            for o in range(4):
                for a in range(2):
                    v = pf[p, a, o]
                    for m in range(3):
                        v = v + rb[p, m, a, o].astype(F32)
                    acc[p, o, a] = v
                    ys[p, o, a] = v.astype(BF16)
            axis_groups.append(send_all(
                yr.at[p],
                [(ys.at[p, mod4(axis + d)], yr.at[p, d - 1], axis_dev(d)) for d in (2, 1, 3)],
            ))
        yield
        x_groups = []
        for p in range(2):
            axis = rings[p][3]
            arrived(axis_groups[p])
            for a in range(2):
                v = acc[p, axis, a]
                for i in range(3):
                    v = v + yr[p, i, a].astype(F32)
                a2[p, a] = v.astype(BF16)
            slot = xr.at[p, myx]
            x_groups.append(send_all(xr.at[p, 0:3], [
                (a2.at[p, 1 - xh], slot, x_far),
                (a2.at[p, 1 - xh], slot, x_pair),
                (a2.at[p, xh], slot, x_same),
            ]))
            xr[p, myx] = a2[p, xh]
        yield
        for p in range(2):
            arrived(x_groups[p])
            terms = [xr[p, i].astype(F32) for i in range(4)]
            out[p] = (terms[0] + terms[1]) + (terms[2] + terms[3])
            yield

    collected = [{}, {}]
    flows = [reduce_scatter(0, q, collected[q]) for q in range(2)]
    for _ in range(3):
        step(flows)
    back = []
    for q in range(2):
        back.append([])
        for p in range(2):
            next(flows[q])
            part = slice(p * 32, p * 32 + 32)
            preact = own_scale[part] * collected[q][p]
            sig = 1.0 / (1.0 + jnp.exp(-preact))
            AS[part, lanes[q]] = (preact * sig).astype(BF16)
            upstream = cot[pl.ds(pl.multiple_of(half + p * 32, 32), 32), lanes[q]].astype(F32)
            grad = upstream * sig * (1.0 + preact * (1.0 - sig))
            XB[q, p, xh, z, y] = (own_scale[part] * grad).astype(BF16)
            back[q].append(all_gather(XB.at[q, p], p))
            step([back[q][p]])
    act_group = send_all(AR, [(AS, AR, sib)])
    for _ in range(2):
        for q in range(2):
            step(back[q])
    act_o[pl.ds(half, 64), :] = AS[...]
    arrived(act_group)
    act_o[pl.ds(other_half, 64), :] = AR[...]

    exchange = [[], []]
    line_q = [functools.partial(back_line, q) for q in range(2)]

    def early_lines(q, d):
        if d:
            step(back[q])
        for k in range(2):
            v = lines_dot(line_q[q], d, k)
            if d:
                v = v + G[1, k, lanes[q]]
            G[1, k, lanes[q]] = v

    def early_exchange(q):
        exchange[q].append(core_sum(G.at[1, :, lanes[q]], GR.at[1, :, lanes[q]]))

    def last_lines(q):
        step(back[q])
        for k in (1, 0):
            v = lines_dot(line_q[q], 1, k)
            LF[k, lanes[q]] = v
            LB[q, k] = v.astype(BF16)
            exchange[q].append(core_sum(LB.at[q, k], LR.at[q, k]))

    weight_terms = []

    def back_messages(q):
        arrived(exchange[q][0])
        for k in range(2):
            early = G[1, k, lanes[q]] + GR[1, 1 - k, lanes[q]]
            arrived(exchange[q][1 + k])
            g = early + (LF[k, lanes[q]] + LR[q, 1 - k].astype(F32))
            if k == 0:
                weight_terms.append(jnp.sum(GATH[lanes[q]] * g, axis=0, keepdims=True))
            MT[1, k, lanes[q], :] = ((SW[k] * INV[k]) * g).astype(BF16)

    for d in (0, 2):
        for q in range(2):
            early_lines(q, d)
    for q in range(2):
        early_lines(q, 3)
        early_exchange(q)
    collected = [{}, {}]
    flows = [reduce_scatter(1, q, collected[q]) for q in range(2)]
    last_lines(0)
    back_messages(0)
    last_lines(1)
    next(flows[0])
    back_messages(1)
    mine = pl.ds(pl.multiple_of(core * 128, 128), 128)
    theirs = pl.ds(pl.multiple_of((1 - core) * 128, 128), 128)
    v = jnp.zeros((128, 256), F32)
    for k in range(2):
        v = v + dot(GH[k, mine, :], MT[1, k], NT) + dot(GL[k, mine, :], MT[1, k], NT)
    T0[...] = v.reshape(4, 4, 8, 256)
    theta_group = send_all(
        TP,
        [(T0.at[mod4(z + a), mod4(y + b)], TP.at[i], plane_dev[i]) for i, (a, b) in enumerate(plane)],
    )
    next(flows[1])
    gw_o[...] = (weight_terms[0] + weight_terms[1]) * INV[0]

    next(flows[0])
    arrived(theta_group)
    v = T0[z, y]
    for i in range(15):
        v = v + TP[i]
    TX[myx] = v
    theta_group = send_all(TX.at[0:3], [(TX.at[myx], TX.at[myx], d) for d in (x_far, x_pair, x_same)])
    next(flows[1])
    next(flows[0])
    arrived(theta_group)
    T3[z, y] = (TX[0] + TX[1]) + (TX[2] + TX[3])
    theta_group = send_all(TP, [(T3.at[z, y], T3.at[z, y], d) for d in plane_dev])
    next(flows[1])
    done = len(groups) - 5
    for g in range(done):
        whole(g).wait_send()
    arrived(theta_group)
    theta_group = send_all(TS, [(T3, TS, sib)])
    gt_o[mine, :] = T3[...].reshape(128, 256)
    arrived(theta_group)
    gt_o[theirs, :] = TS[...].reshape(128, 256)
    for p in range(2):
        step(flows)
        part = slice(p * 32, p * 32 + 32)
        proj = jnp.concatenate([own_scale[part] * collected[q][p] for q in range(2)], axis=1)
        hi, lo = split(proj)
        FS[part, :] = (dot(hi, theta[...], NT) + dot(lo, theta[...], NT)).astype(BF16)
    grad_group = send_all(FR, [(FS, FR, sib)])
    gf_o[pl.ds(half, 64), :] = FS[...]
    arrived(grad_group)
    gf_o[pl.ds(other_half, 64), :] = FR[...]
    assert len(groups) == N_SEM, len(groups)
    for g in range(done, len(groups)):
        whole(g).wait_send()


def write_out(a, b, c, d, a_o, b_o, c_o, d_o, sem):
    pairs = [(a, a_o), (b, b_o), (c, c_o), (d, d_o)]
    copies = [pltpu.make_async_copy(src, dst, sem.at[i]) for i, (src, dst) in enumerate(pairs)]
    for copy in copies:
        copy.start()
    for copy in copies:
        copy.wait()


def body(features, theta, section_weight, pair_rows, pair_cols, pair_counts, cotangent):
    vmem = pl.BlockSpec(memory_space=pltpu.VMEM)
    hbm = pl.BlockSpec(memory_space=pltpu.HBM)

    def buf(shape, dtype):
        return pltpu.VMEM(shape, dtype)

    ins = (features, theta, section_weight.reshape(1, -1), pair_rows, pair_cols, pair_counts, cotangent)
    ins = [pltpu.with_memory_space_constraint(v, pltpu.HBM) for v in ins]
    outs = pl.pallas_call(
        layer,
        out_shape=(
            jax.ShapeDtypeStruct((128, 256), BF16),
            jax.ShapeDtypeStruct((128, 256), BF16),
            jax.ShapeDtypeStruct((256, 256), F32),
            jax.ShapeDtypeStruct((1, 512), F32),
        ),
        in_specs=[hbm] * 7,
        out_specs=(vmem, vmem, vmem, vmem),
        scratch_shapes=[
            buf((128, 256), BF16),
            buf((256, 256), BF16),
            buf((32, 512), jnp.int32),
            buf((32, 512), jnp.int32),
            pltpu.SMEM((1, 32), jnp.int32),
            buf((128, 256), BF16),
            buf((2, 2, 2, 4, 4, 32, 512), BF16),
            buf((2, 2, 4, 4, 32, 512), BF16),
            buf((8, 512), F32),
            buf((8, 512), F32),
            buf((16, 128), F32),
            buf((3, 16, 128), F32),
            buf((16, 128), F32),
            buf((15, 16, 128), F32),
            buf((128, 128), F32),
            buf((128, 128), F32),
            buf((2, 1, 512), F32),
            buf((2, 1, 512), F32),
            buf((2, 2, 4, 4, 32, 256), BF16),
            buf((2, 2, 2, 4, 4, 32, 128), BF16),
            buf((2, 2, 4, 4, 32, 128), F32),
            buf((2, 2, 272, 512), F32),
            buf((2, 2, 272, 512), F32),
            buf((2, 256, 512), F32),
            buf((2, 2, 128, 512), BF16),
            buf((2, 2, 128, 512), BF16),
            buf((2, 256, 512), BF16),
            buf((2, 256, 512), BF16),
            buf((256, 512), F32),
            buf((2, 2, 256, 512), BF16),
            buf((2, 2, 2, 4, 32, 128), F32),
            buf((2, 2, 2, 3, 2, 4, 32, 128), BF16),
            buf((2, 2, 2, 3, 2, 4, 32, 128), BF16),
            buf((2, 2, 4, 2, 32, 128), F32),
            buf((2, 2, 2, 4, 2, 32, 128), BF16),
            buf((2, 2, 2, 3, 2, 32, 128), BF16),
            buf((2, 2, 2, 2, 32, 128), BF16),
            buf((2, 2, 2, 4, 32, 128), BF16),
            buf((64, 256), BF16),
            buf((64, 256), BF16),
            buf((64, 256), BF16),
            buf((64, 256), BF16),
            buf((256, 256), BF16),
            buf((4, 4, 8, 256), F32),
            buf((15, 8, 256), F32),
            buf((4, 8, 256), F32),
            buf((4, 4, 8, 256), F32),
            buf((4, 4, 8, 256), F32),
            pltpu.SemaphoreType.DMA((N_SEM,)),
            pltpu.SemaphoreType.DMA((N_SEM,)),
            pltpu.SemaphoreType.DMA((7,)),
        ],
        compiler_params=pltpu.CompilerParams(
            collective_id=0, has_side_effects=True, vmem_limit_bytes=40 * 1024 * 1024
        ),
    )(*ins)
    anywhere = pl.BlockSpec(memory_space=pl.ANY)
    outs = pl.pallas_call(
        write_out,
        out_shape=tuple(jax.ShapeDtypeStruct(o.shape, o.dtype) for o in outs),
        in_specs=[vmem] * 4,
        out_specs=(anywhere,) * 4,
        scratch_shapes=[pltpu.SemaphoreType.DMA((4,))],
        compiler_params=pltpu.CompilerParams(vmem_limit_bytes=4 * 1024 * 1024),
    )(*outs)
    return outs[0], outs[1], outs[2], outs[3].reshape(-1)


def solution(mesh):
    placed = (
        P("ent", None),
        P(),
        P(("ent", "sec")),
        P(("ent", "sec"), None, None),
        P(("ent", "sec"), None, None),
        P(("ent", "sec"), None),
        P("ent", None),
    )
    return jax.shard_map(
        body,
        mesh=mesh,
        in_specs=placed,
        out_specs=(P("ent", None), P("ent", None), P(), P(("ent", "sec"))),
        check_vma=False,
    )
```
